128 devices in a mesh: chan: 16 (over x_hi, z, core), tm: 8 (over x_lo, y).
Axes of the slice: x: 4 (x_hi: 2, x_lo: 2; x = x_hi * 2 + x_lo), y: 4, z: 4, core: 2. Of those that a mesh axis runs over, the one named last changes fastest.
Arguments:
- traces: float32 [512, 131072], P('chan', 'tm'), may hold values from -8 to 8
- live_channel: int32 [512], P('chan'), may hold values 0 or 1
- valid_segment: int32 [512, 512], P('chan', 'tm'), may hold values 0 or 1
Outputs:
- correlation: float32 [512, 512, 256], P('chan', 'tm')
The draws below stay inside these ranges and needn't reach their ends.
All inputs are finite; a program needn't handle non-finite values. No bound on the sum of `live_channel` or of `valid_segment` on one device may be relied on, other than what follows from the above.
Results may differ from the reference program's by a relative error of at most 0.003.
Values may be sent and summed in bfloat16 or wider, within the bound.
No kernel may reach another device: no remote copies, remote signals or barrier semaphores. Data moves between devices by JAX's collectives and lax.ppermute only.
A program may use at most 192 MiB of HBM per device.

```python
import jax
import jax.numpy as jnp
from jax import lax

SEG_LEN = 256
BINS = 128
HALF_WIN = 64
SMOOTH = 4
CHANNELS = 512
SEGMENTS = 512
SAMPLES = 131072


def with_ends(result, own_key, low, high):
    extent = result.shape
    index_at = [jax.random.randint(jax.random.fold_in(own_key, axis), (), 0, extent[axis]) for axis in range(len(extent))]
    result = result.at[tuple(index_at)].set(low)
    longest = extent.index(max(extent))
    index_at[longest] = (index_at[longest] + 1) % extent[longest]
    return result.at[tuple(index_at)].set(high)


def shard_levels(own_key, dims, shards, smallest, largest):
    def one(dim, blocks):
        heights = jax.random.uniform(jax.random.fold_in(jax.random.fold_in(own_key, 6), dim), (blocks,), jnp.float32, smallest / len(shards), largest / len(shards))
        return jnp.repeat(jnp.exp(heights), dims[dim] // blocks).reshape((-1,) + (1,) * (len(dims) - dim - 1))

    loudness = one(*shards[0])
    for cut in shards[1:]:
        loudness = loudness * one(*cut)
    return loudness


def bell_draw(rng, shape, scale, reach, pieces=(), kind=jnp.bfloat16):
    values = jax.random.normal(rng, shape, jnp.float32) * scale
    if len(pieces) > 0:
        values = shard_levels(rng, shape, pieces, -0.22, 0.18) * values
    return jnp.clip(values, min=-reach, max=reach).astype(kind)


def setup_inputs(seed: int = 0) -> dict:
    seeds = jax.random.split(jax.random.key(seed), 4)
    return {
        "traces": bell_draw(seeds[0], (CHANNELS, SAMPLES), 1.0, 8.0, ((0, 16), (1, 8)), jnp.float32),
        "live_channel": with_ends((jax.random.randint(seeds[1], (CHANNELS,), 0, 16) < 15).astype(jnp.int32), jax.random.fold_in(seeds[1], 1), 0, 1),
        "valid_segment": with_ends((jax.random.randint(seeds[2], (CHANNELS, SEGMENTS), 0, 8) < 7).astype(jnp.int32), jax.random.fold_in(seeds[2], 1), 0, 1),
    }


def make_tables():
    length = SEG_LEN
    times_col = jnp.arange(length, dtype=jnp.int32)[:, None]
    freq_row = jnp.arange(BINS, dtype=jnp.int32)[None, :]
    phase = 2.0 * jnp.pi / length * (times_col * freq_row % length).astype(jnp.float32)
    forward_table = jnp.concatenate([jnp.cos(phase), -jnp.sin(phase)], axis=1)
    freq_col = jnp.arange(BINS, dtype=jnp.int32)[:, None]
    lag_row = jnp.arange(length, dtype=jnp.int32)[None, :] - BINS
    back_phase = 2.0 * jnp.pi / length * (freq_col * lag_row % length).astype(jnp.float32)
    inverse_table = jnp.concatenate([jnp.cos(back_phase), -jnp.sin(back_phase)], axis=0)
    bin_a = jnp.arange(BINS, dtype=jnp.int32)[:, None]
    bin_b = jnp.arange(BINS, dtype=jnp.int32)[None, :]
    smooth_table = (jnp.abs(bin_a - bin_b) <= SMOOTH).astype(jnp.float32) / (2.0 * SMOOTH + 1.0)
    bandpass = (jnp.arange(BINS, dtype=jnp.int32) > 0).astype(jnp.float32)
    return (forward_table, inverse_table, smooth_table, bandpass)

def reference(traces, live_channel, valid_segment):
    forward_table, inverse_table, smooth_table, bandpass = make_tables()
    highest = lax.Precision.HIGHEST
    padded = jnp.pad(jnp.abs(traces), ((0, 0), (HALF_WIN, HALF_WIN)))
    window_sum = lax.reduce_window(padded, jnp.zeros((), padded.dtype), lax.add, (1, 2 * HALF_WIN + 1), (1, 1), 'VALID')
    abs_level = window_sum / (2.0 * HALF_WIN + 1.0)
    normed = traces / (abs_level + 1e-05)
    segments = normed.reshape(CHANNELS, SEGMENTS, SEG_LEN)
    spectrum = jnp.dot(segments, forward_table, precision=highest, preferred_element_type=jnp.float32)
    spectrum = spectrum.reshape(CHANNELS, SEGMENTS, 2, BINS)
    spectral_power = spectrum[:, :, 0] ** 2 + spectrum[:, :, 1] ** 2
    smoothed = jnp.dot(spectral_power, smooth_table, precision=highest, preferred_element_type=jnp.float32)
    mean_power = lax.optimization_barrier(jnp.mean(spectral_power, axis=-1, keepdims=True))
    seg_mask = (live_channel[:, None] * valid_segment).astype(jnp.bfloat16)
    whiten_scale = bandpass * seg_mask.astype(jnp.float32)[:, :, None] / jnp.sqrt(smoothed + 0.1 * mean_power + 1e-06)
    whitened = (spectrum * whiten_scale[:, :, None, :]).astype(jnp.bfloat16)
    pair_count = jnp.dot(seg_mask, seg_mask.T, preferred_element_type=jnp.float32)
    local_white = whitened.astype(jnp.float32)
    turned = jnp.stack([local_white[:, :, 1], -local_white[:, :, 0]], axis=2)
    cross_real = jnp.einsum('iscf,jscf->ijf', local_white, local_white, precision=highest)
    cross_imag = jnp.einsum('iscf,jscf->ijf', local_white, turned, precision=highest)
    cross = jnp.stack([cross_real, cross_imag], axis=2).reshape(CHANNELS, CHANNELS, 2 * BINS)
    lagged = jnp.dot(cross, inverse_table, precision=highest, preferred_element_type=jnp.float32)
    return lagged * (2.0 / jnp.maximum(pair_count, 1.0))[:, :, None]
```

```python
import jax
import jax.numpy as jnp
from jax import lax
from jax.sharding import PartitionSpec as P

SEG_LEN = 256
BINS = 128
HALF_WIN = 64
SMOOTH = 4
ALL = ("chan", "tm")


def with_halo(array, sides, width):
    for axis, dim in sides:
        count, length = (lax.axis_size(axis), array.shape[dim])
        up = [(i, (i + 1) % count) for i in range(count - 1)]
        down = [(j, i) for i, j in up]
        last = lax.slice_in_dim(array, length - width, length, axis=dim)
        first = lax.slice_in_dim(array, 0, width, axis=dim)
        before = lax.ppermute(last, axis, up)
        after = lax.ppermute(first, axis, down)
        array = jnp.concatenate([before, array, after], axis=dim)
    return array


def make_tables():
    length = SEG_LEN
    times_col = jnp.arange(length, dtype=jnp.int32)[:, None]
    freq_row = jnp.arange(BINS, dtype=jnp.int32)[None, :]
    phase = 2.0 * jnp.pi / length * (times_col * freq_row % length).astype(jnp.float32)
    forward_table = jnp.concatenate([jnp.cos(phase), -jnp.sin(phase)], axis=1)
    freq_col = jnp.arange(BINS, dtype=jnp.int32)[:, None]
    lag_row = jnp.arange(length, dtype=jnp.int32)[None, :] - BINS
    back_phase = 2.0 * jnp.pi / length * (freq_col * lag_row % length).astype(jnp.float32)
    bandpass = (jnp.arange(BINS, dtype=jnp.int32) > 0).astype(jnp.float32)
    inverse_table = jnp.stack([jnp.cos(back_phase), -jnp.sin(back_phase)], axis=1)
    inverse_table = inverse_table * bandpass[:, None, None]
    bin_a = jnp.arange(BINS, dtype=jnp.int32)[:, None]
    bin_b = jnp.arange(BINS, dtype=jnp.int32)[None, :]
    smooth_table = (jnp.abs(bin_a - bin_b) <= SMOOTH).astype(jnp.float32) / (2.0 * SMOOTH + 1.0)
    sample_in = jnp.arange(SEG_LEN + 2 * HALF_WIN, dtype=jnp.int32)[:, None]
    sample_out = jnp.arange(SEG_LEN, dtype=jnp.int32)[None, :]
    inside = (sample_in >= sample_out) & (sample_in <= sample_out + 2 * HALF_WIN)
    box_table = inside.astype(jnp.float32) / (2.0 * HALF_WIN + 1.0)
    return (forward_table, inverse_table, smooth_table, bandpass, box_table)


def body(traces, live_channel, valid_segment):
    forward_table, inverse_table, smooth_table, bandpass, box_table = make_tables()
    highest = lax.Precision.HIGHEST
    chan_rows = traces.shape[0]
    seg_count = valid_segment.shape[1]
    span = seg_count * SEG_LEN
    chans, slabs = lax.axis_size("chan"), lax.axis_size("tm")
    magnitude = jnp.abs(traces)
    slab_ends = jnp.concatenate([magnitude[:, :HALF_WIN], magnitude[:, span - HALF_WIN :]], axis=1)
    rims = with_halo(slab_ends, (("tm", 1),), HALF_WIN)
    padded = jnp.concatenate(
        [rims[:, :HALF_WIN], magnitude, rims[:, rims.shape[1] - HALF_WIN :]], axis=1
    )
    head_part = padded[:, :span].reshape(chan_rows, seg_count, SEG_LEN)
    extended = jnp.pad(padded, ((0, 0), (0, SEG_LEN - 2 * HALF_WIN)))
    tail_part = extended[:, SEG_LEN : SEG_LEN + span].reshape(chan_rows, seg_count, SEG_LEN)[
        :, :, : 2 * HALF_WIN
    ]
    window = jnp.concatenate([head_part, tail_part], axis=2)
    abs_level = jnp.dot(window, box_table, precision=highest, preferred_element_type=jnp.float32)
    normed = traces.reshape(chan_rows, seg_count, SEG_LEN) / (abs_level + 1e-05)
    spectrum = jnp.dot(normed, forward_table, precision=highest, preferred_element_type=jnp.float32)
    spectrum = spectrum.reshape(chan_rows, seg_count, 2, BINS)
    spectral_power = spectrum[:, :, 0] ** 2 + spectrum[:, :, 1] ** 2
    smoothed = jnp.dot(
        spectral_power, smooth_table, precision=highest, preferred_element_type=jnp.float32
    )
    mean_power = jnp.mean(spectral_power, axis=-1, keepdims=True)
    seg_mask = (live_channel[:, None] * valid_segment).astype(jnp.float32)
    whiten_scale = (
        bandpass * seg_mask[:, :, None] / jnp.sqrt(smoothed + 0.1 * mean_power + 1e-06)
    )
    whitened = spectrum * whiten_scale[:, :, None, :]
    carries = jnp.zeros((2, BINS), jnp.float32).at[0, 0].set(1.0)
    whitened = (whitened + seg_mask[:, :, None, None] * carries).astype(jnp.bfloat16)
    sent = jnp.transpose(whitened, (3, 0, 2, 1)).reshape(BINS, chan_rows, 2 * seg_count)
    got = lax.all_to_all(sent, ALL, 0, 0, tiled=True)
    got = got.reshape(chans, slabs, chan_rows, 2, seg_count)
    spec = jnp.transpose(got, (0, 2, 1, 3, 4)).reshape(chans * chan_rows, slabs, 2, seg_count)
    turned = jnp.stack([spec[:, :, 1], -spec[:, :, 0]], axis=2)
    flat = spec.reshape(chans * chan_rows, -1)
    cross_real = jnp.dot(flat, flat.T, preferred_element_type=jnp.float32)
    cross_imag = jnp.dot(
        flat, turned.reshape(chans * chan_rows, -1).T, preferred_element_type=jnp.float32
    )
    rounded = lax.reduce_precision(cross_real, 8, 7)
    is_count = (lax.axis_index(ALL) == 0)
    cross_imag = jnp.where(is_count, cross_real - rounded, cross_imag)
    cols = (chans * chan_rows) // slabs
    pieces = jnp.stack([rounded, cross_imag], axis=0).astype(jnp.bfloat16)
    pieces = pieces.reshape(2, chans, chan_rows, slabs, cols)
    pieces = jnp.transpose(pieces, (1, 3, 2, 0, 4)).reshape(BINS, chan_rows, 2 * cols)
    back = lax.all_to_all(pieces, ALL, 0, 0, tiled=True)
    back = back.reshape(BINS, chan_rows, 2, cols).astype(jnp.float32)
    count = back[0, :, 0] + back[0, :, 1]
    lagged = jnp.einsum(
        "fikj,fkl->ijl", back, inverse_table, precision=highest, preferred_element_type=jnp.float32
    )
    return lagged * (2.0 / jnp.maximum(count, 1.0))[:, :, None]


def solution(mesh):
    return jax.shard_map(
        body,
        mesh=mesh,
        in_specs=(P("chan", "tm"), P("chan"), P("chan", "tm")),
        out_specs=P("chan", "tm", None),
        check_vma=False,
    )
```

```python
import jax
import jax.numpy as jnp
import numpy as np
from jax import lax
from jax.experimental import pallas as pl
from jax.experimental.pallas import tpu as pltpu
from jax.sharding import PartitionSpec as P

SEG_LEN = 256
BINS = 128
HALF_WIN = 64
SMOOTH = 4
LANES = 128
ALL = ("chan", "tm")
F32 = jnp.float32
BF16 = jnp.bfloat16
VMEM = pl.BlockSpec(memory_space=pltpu.VMEM)


def split(table):
    high = table.astype(BF16)
    low = (table - high.astype(np.float32)).astype(BF16)
    return high, low


def front_tables():
    t_in = np.arange(SEG_LEN)[:, None]
    t_out = np.arange(SEG_LEN)[None, :]
    box_mid = (np.abs(t_in - t_out) <= HALF_WIN).astype(BF16)
    edge = np.arange(LANES)[:, None]
    edge = np.where(edge < HALF_WIN, SEG_LEN + edge, edge - LANES)
    box_edge = (np.abs(edge - t_out) <= HALF_WIN).astype(BF16)
    phase = 2.0 * np.pi / SEG_LEN * (t_in * np.arange(BINS)[None, :] % SEG_LEN)
    forward = np.concatenate([np.cos(phase), -np.sin(phase)], axis=1).astype(np.float32)
    bins = np.arange(BINS)
    band = (np.abs(bins[:, None] - bins[None, :]) <= SMOOTH).astype(BF16)
    band = np.concatenate([band, np.ones((BINS, BINS), BF16)], axis=1)
    return (box_mid, box_edge, *split(forward), band)


def inverse_tables():
    freq = np.arange(BINS)[:, None]
    lag = np.arange(SEG_LEN)[None, :] - BINS
    phase = 2.0 * np.pi / SEG_LEN * (freq * lag % SEG_LEN)
    table = np.stack([np.cos(phase), -np.sin(phase)], axis=1) * (freq > 0)[:, None, :]
    return table.astype(np.float32)


def mxu(a, b):
    return jnp.dot(a, b, preferred_element_type=F32)


def halves(x):
    high = x.astype(BF16)
    return high, (x - high.astype(F32)).astype(BF16)


def front_kernel(
    x_ref, before_ref, after_ref, live_ref, valid_ref,
    mid_ref, edge_ref, high_ref, low_ref, band_ref,
    out_ref, re_ref, im_ref, turned_ref,
):
    rows, span = x_ref.shape
    segs = span // SEG_LEN
    group = 8
    lane = lax.broadcasted_iota(jnp.int32, (rows, LANES), 1)
    first = lax.broadcasted_iota(jnp.int32, (group * rows, BINS), 1) == 0
    for g in range(segs // group):
        own, rim = [], []
        for s in range(g * group, (g + 1) * group):
            start = s * SEG_LEN
            stop = start + SEG_LEN
            own.append(x_ref[:, start:stop])
            left = x_ref[:, start - LANES : start] if s > 0 else before_ref[...]
            right = x_ref[:, stop : stop + LANES] if s < segs - 1 else after_ref[...]
            rim.append(jnp.where(lane < HALF_WIN, right, left))
        x = jnp.concatenate(own, axis=0)
        a_high, a_low = halves(jnp.abs(x))
        e_high, e_low = halves(jnp.abs(jnp.concatenate(rim, axis=0)))
        mid, edge = mid_ref[...], edge_ref[...]
        total = mxu(a_high, mid) + mxu(a_low, mid) + mxu(e_high, edge) + mxu(e_low, edge)
        n_high, n_low = halves(x / (total * (1.0 / (2 * HALF_WIN + 1)) + 1e-05))
        table = high_ref[...]
        spec = mxu(n_high, table) + mxu(n_low, table) + mxu(n_high, low_ref[...])
        re, im = spec[:, :BINS], spec[:, BINS:]
        p_high, p_low = halves(re * re + im * im)
        sums = mxu(p_high, band_ref[...]) + mxu(p_low, band_ref[...])
        floor = sums[:, :BINS] * (1.0 / (2 * SMOOTH + 1)) + sums[:, BINS:] * (0.1 / BINS)
        scale = lax.rsqrt(floor + 1e-06)
        at = pl.ds(g * group * rows, group * rows)
        re_ref[at, :] = jnp.where(first, 1.0, re * scale)
        im_ref[at, :] = jnp.where(first, 0.0, im * scale)
    for c in range(rows):
        picked = pl.ds(c, segs, stride=rows)
        both = jnp.concatenate([re_ref[picked, :], im_ref[picked, :]], axis=0)
        turned_ref[pl.ds(c, BINS, stride=rows), :] = both.T
    mask = (live_ref[...] * valid_ref[...]).astype(F32)
    mask = jnp.concatenate([mask, mask], axis=1)
    whitened = turned_ref[...].reshape(BINS, rows, LANES) * mask[None]
    out_ref[...] = whitened.astype(BF16)


def front(traces, before, after, live, valid):
    rows, span = traces.shape
    segs = span // SEG_LEN
    return pl.pallas_call(
        front_kernel,
        out_shape=jax.ShapeDtypeStruct((BINS, rows, 2 * segs), BF16),
        in_specs=[VMEM] * 10,
        out_specs=VMEM,
        scratch_shapes=[
            pltpu.VMEM((segs * rows, BINS), F32),
            pltpu.VMEM((segs * rows, BINS), F32),
            pltpu.VMEM((BINS * rows, LANES), F32),
        ],
        compiler_params=pltpu.CompilerParams(vmem_limit_bytes=32 << 20),
        name="front",
    )(traces, before, after, live[:, None], valid, *front_tables())


def cross_kernel(got_ref, out_ref, x_ref, r_ref):
    chans, slabs, rows, _ = got_ref.shape
    cols = chans * rows // slabs
    half = LANES // 2
    lane = lax.broadcasted_iota(jnp.int32, (chans * rows, LANES), 1)
    sign = jnp.where(lane < half, 1.0, -1.0)
    for t in range(slabs):
        tile = got_ref[:, t].reshape(chans * rows, LANES)
        turned = (pltpu.roll(tile.astype(F32), half, 1) * sign).astype(BF16)
        at = slice(t * LANES, (t + 1) * LANES)
        x_ref[:, at] = tile
        for u in range(slabs):
            r_ref[2 * u * cols : (2 * u + 1) * cols, at] = tile[u * cols : (u + 1) * cols]
            r_ref[(2 * u + 1) * cols : (2 * u + 2) * cols, at] = turned[u * cols : (u + 1) * cols]
    holds_count = lax.axis_index("chan") * lax.axis_size("tm") + lax.axis_index("tm") == 0
    x = x_ref[...]
    for u in range(0, slabs, 2):
        r = r_ref[2 * u * cols : (2 * u + 4) * cols, :]
        cross = lax.dot_general(x, r, (((1,), (1,)), ((), ())), preferred_element_type=F32)
        for v in range(2):
            part = cross[:, v * LANES : (v + 1) * LANES]
            high = part.astype(BF16)
            out_ref[:, u + v] = high.reshape(chans, rows, LANES)

            @pl.when(holds_count)
            def _():
                whole = high.astype(F32)
                both = whole + pltpu.roll(part - whole, half, 1)
                out_ref[:, u + v] = both.astype(BF16).reshape(chans, rows, LANES)


def cross_spectra(got):
    chans, slabs, rows, lanes = got.shape
    return pl.pallas_call(
        cross_kernel,
        out_shape=jax.ShapeDtypeStruct(got.shape, BF16),
        in_specs=[VMEM],
        out_specs=VMEM,
        scratch_shapes=[
            pltpu.VMEM((chans * rows, slabs * lanes), BF16),
            pltpu.VMEM((2 * chans * rows, slabs * lanes), BF16),
        ],
        compiler_params=pltpu.CompilerParams(vmem_limit_bytes=32 << 20),
        name="cross_spectra",
    )(got)


def body(traces, live_channel, valid_segment):
    span = traces.shape[1]
    chans, slabs = lax.axis_size("chan"), lax.axis_size("tm")
    up = [(i, i + 1) for i in range(slabs - 1)]
    down = [(j, i) for i, j in up]
    before = lax.ppermute(traces[:, span - LANES :], "tm", up)
    after = lax.ppermute(traces[:, :LANES], "tm", down)
    sent = front(traces, before, after, live_channel, valid_segment)
    got = lax.all_to_all(sent, ALL, 0, 0, tiled=True)
    pieces = cross_spectra(got.reshape(chans, slabs, *got.shape[1:]))
    back = lax.all_to_all(pieces.reshape(got.shape), ALL, 0, 0, tiled=True)
    rows, cols = back.shape[1], back.shape[2] // 2
    back = back.reshape(BINS, rows, 2, cols).astype(F32)
    count = back[0, :, 0] + back[0, :, 1]
    lagged = jnp.einsum(
        "fikj,fkl->ijl",
        back,
        jnp.asarray(inverse_tables()),
        precision=lax.Precision.HIGHEST,
        preferred_element_type=F32,
    )
    return lagged * (2.0 / jnp.maximum(count, 1.0))[:, :, None]


def solution(mesh):
    return jax.shard_map(
        body,
        mesh=mesh,
        in_specs=(P("chan", "tm"), P("chan"), P("chan", "tm")),
        out_specs=P("chan", "tm", None),
        check_vma=False,
    )
```

```python
import jax
import jax.numpy as jnp
import numpy as np
from jax import lax
from jax.experimental import pallas as pl
from jax.experimental.pallas import tpu as pltpu
from jax.sharding import PartitionSpec as P

SEG_LEN = 256
BINS = 128
HALF_WIN = 64
SMOOTH = 4
LANES = 128
ALL = ("chan", "tm")
F32 = jnp.float32
BF16 = jnp.bfloat16
VMEM = pl.BlockSpec(memory_space=pltpu.VMEM)


def split(table):
    high = table.astype(BF16)
    low = (table - high.astype(np.float32)).astype(BF16)
    return high, low


def front_tables():
    t_in = np.arange(SEG_LEN)[:, None]
    t_out = np.arange(SEG_LEN)[None, :]
    box_mid = (np.abs(t_in - t_out) <= HALF_WIN).astype(BF16)
    edge = np.arange(LANES)[:, None]
    edge = np.where(edge < HALF_WIN, SEG_LEN + edge, edge - LANES)
    box_edge = (np.abs(edge - t_out) <= HALF_WIN).astype(BF16)
    phase = 2.0 * np.pi / SEG_LEN * (t_in * np.arange(BINS)[None, :] % SEG_LEN)
    forward = np.concatenate([np.cos(phase), -np.sin(phase)], axis=1).astype(np.float32)
    bins = np.arange(BINS)
    band = (np.abs(bins[:, None] - bins[None, :]) <= SMOOTH).astype(BF16)
    band = np.concatenate([band, np.ones((BINS, BINS), BF16)], axis=1)
    return np.stack([box_mid, np.tile(box_edge, (2, 1)), *split(forward), np.tile(band, (2, 1))])


def inverse_tables():
    freq = np.arange(BINS)[:, None]
    lag = np.arange(SEG_LEN)[None, :] - BINS
    phase = 2.0 * np.pi / SEG_LEN * (freq * lag % SEG_LEN)
    table = np.stack([np.cos(phase), -np.sin(phase)], axis=1) * (freq > 0)[:, None, :]
    return table.astype(np.float32)


def mxu(a, b):
    return jnp.dot(a, b, preferred_element_type=F32)


def halves(x):
    high = x.astype(BF16)
    return high, (x - high.astype(F32)).astype(BF16)


def whiten(x, rim, table_ref):
    mid, edge, high, low, band = (table_ref[i] for i in range(5))
    a_high, a_low = halves(jnp.abs(x))
    e_both = jnp.concatenate(halves(jnp.abs(rim)), axis=1)
    total = mxu(a_high, mid) + mxu(a_low, mid) + mxu(e_both, edge)
    n_high, n_low = halves(x / (total * (1.0 / (2 * HALF_WIN + 1)) + 1e-05))
    spec = mxu(n_high, high) + mxu(n_low, high) + mxu(n_high, low)
    re, im = spec[:, :BINS], spec[:, BINS:]
    sums = mxu(jnp.concatenate(halves(re * re + im * im), axis=1), band)
    floor = sums[:, :BINS] * (1.0 / (2 * SMOOTH + 1)) + sums[:, BINS:] * (0.1 / BINS)
    scale = lax.rsqrt(floor + 1e-06)
    first = lax.broadcasted_iota(jnp.int32, re.shape, 1) == 0
    return jnp.where(first, 1.0, re * scale), jnp.where(first, 0.0, im * scale)


def beside(right, left):
    lane = lax.broadcasted_iota(jnp.int32, right.shape, 1)
    return jnp.where(lane < HALF_WIN, right, left)


GROUP = 8
END = SEG_LEN + LANES


def spectra_kernel(x_hbm, table_hbm, re_ref, im_ref, ends_ref, x_ref, table_ref, sems):
    rows, span = x_ref.shape
    segs = span // SEG_LEN
    width = GROUP * SEG_LEN
    groups = span // width
    copies = [
        pltpu.make_async_copy(
            x_hbm.at[:, g * width : (g + 1) * width],
            x_ref.at[:, g * width : (g + 1) * width],
            sems.at[g],
        )
        for g in range(groups)
    ]
    table_copy = pltpu.make_async_copy(table_hbm, table_ref, sems.at[groups])
    copies[0].start()
    table_copy.start()
    for copy in copies[1:]:
        copy.start()
    copies[0].wait()
    table_copy.wait()
    nothing = jnp.zeros((rows, LANES), F32)
    for g in range(groups):
        if g + 1 < groups:
            copies[g + 1].wait()
        own, rim = [], []
        for s in range(g * GROUP, (g + 1) * GROUP):
            start = s * SEG_LEN
            stop = start + SEG_LEN
            own.append(x_ref[:, start:stop])
            left = x_ref[:, start - LANES : start] if s > 0 else nothing
            right = x_ref[:, stop : stop + LANES] if s < segs - 1 else nothing
            rim.append(beside(right, left))
        re, im = whiten(jnp.concatenate(own, axis=0), jnp.concatenate(rim, axis=0), table_ref)
        at = slice(g * GROUP * rows, (g + 1) * GROUP * rows)
        re_ref[at, :] = re
        im_ref[at, :] = im
    ends_ref[:, :END] = x_ref[:, :END]
    ends_ref[:, END:] = x_ref[:, span - END :]


def spectra(traces, table):
    rows, span = traces.shape
    segs = span // SEG_LEN
    half = jax.ShapeDtypeStruct((segs * rows, BINS), F32)
    return pl.pallas_call(
        spectra_kernel,
        out_shape=(half, half, jax.ShapeDtypeStruct((rows, 2 * END), F32)),
        in_specs=[pl.BlockSpec(memory_space=pltpu.HBM)] * 2,
        out_specs=(VMEM, VMEM, VMEM),
        scratch_shapes=[
            pltpu.VMEM(traces.shape, F32),
            pltpu.VMEM(table.shape, BF16),
            pltpu.SemaphoreType.DMA((span // (GROUP * SEG_LEN) + 1,)),
        ],
        compiler_params=pltpu.CompilerParams(vmem_limit_bytes=32 << 20),
        name="spectra",
    )(
        pltpu.with_memory_space_constraint(traces, pltpu.HBM),
        pltpu.with_memory_space_constraint(table, pltpu.HBM),
    )


def turn_kernel(
    re_ref, im_ref, ends_ref, before_ref, after_ref, live_ref, valid_ref, table_ref,
    out_ref, turned_ref,
):
    rows = ends_ref.shape[0]
    segs = re_ref.shape[0] // rows
    x = jnp.concatenate([ends_ref[:, :SEG_LEN], ends_ref[:, END + LANES :]], axis=0)
    rim = [
        beside(ends_ref[:, SEG_LEN:END], before_ref[...]),
        beside(after_ref[...], ends_ref[:, END : END + LANES]),
    ]
    fixed = whiten(x, jnp.concatenate(rim, axis=0), table_ref)
    row = lax.broadcasted_iota(jnp.int32, (8, BINS), 0)
    for c in range(rows):
        pieces = []
        for ref, ends in zip((re_ref, im_ref), fixed):
            picked = ref[pl.ds(c, segs, stride=rows), :]
            pieces += [
                jnp.where(row == 0, ends[c : c + 1], picked[:8]),
                picked[8 : segs - 8],
                jnp.where(row == 7, ends[rows + c : rows + c + 1], picked[segs - 8 :]),
            ]
        turned_ref[pl.ds(c, BINS, stride=rows), :] = jnp.concatenate(pieces, axis=0).T
    live = jnp.broadcast_to(live_ref[...].astype(F32), (rows, rows))
    here = [lax.broadcasted_iota(jnp.int32, (rows, rows), axis) for axis in range(2)]
    live = jnp.sum(jnp.where(here[0] == here[1], live, 0.0), axis=1, keepdims=True)
    mask = live * valid_ref[...].astype(F32)
    mask = jnp.concatenate([mask, mask], axis=1)
    whitened = turned_ref[...].reshape(BINS, rows, LANES) * mask[None]
    out_ref[...] = whitened.astype(BF16)


def turn(parts, before, after, live, valid, table):
    rows, segs = valid.shape
    return pl.pallas_call(
        turn_kernel,
        out_shape=jax.ShapeDtypeStruct((BINS, rows, 2 * segs), BF16),
        in_specs=[VMEM] * 8,
        out_specs=VMEM,
        scratch_shapes=[pltpu.VMEM((BINS * rows, LANES), F32)],
        compiler_params=pltpu.CompilerParams(vmem_limit_bytes=32 << 20),
        name="turn",
    )(*parts, before, after, live[None, :], valid, table)


def front(traces, before, after, live, valid):
    table = jnp.asarray(front_tables())
    return turn(spectra(traces, table), before, after, live, valid, table)


def cross_kernel(got_ref, out_ref, x_ref, r_ref):
    chans, slabs, rows, _ = got_ref.shape
    cols = chans * rows // slabs
    half = LANES // 2
    lane = lax.broadcasted_iota(jnp.int32, (chans * rows, LANES), 1)
    sign = jnp.where(lane < half, 1.0, -1.0)
    for t in range(slabs):
        tile = got_ref[:, t].reshape(chans * rows, LANES)
        turned = (pltpu.roll(tile.astype(F32), half, 1) * sign).astype(BF16)
        at = slice(t * LANES, (t + 1) * LANES)
        x_ref[:, at] = tile
        for u in range(slabs):
            r_ref[2 * u * cols : (2 * u + 1) * cols, at] = tile[u * cols : (u + 1) * cols]
            r_ref[(2 * u + 1) * cols : (2 * u + 2) * cols, at] = turned[u * cols : (u + 1) * cols]
    middle = slabs // 2 * LANES

    @pl.when(lax.axis_index("chan") * lax.axis_size("tm") + lax.axis_index("tm") == 0)
    def _():
        for u in range(slabs):
            real = slice(2 * u * cols, (2 * u + 1) * cols)
            imag = slice((2 * u + 1) * cols, (2 * u + 2) * cols)
            own = slice(u * cols, (u + 1) * cols)
            r_ref[real, middle:] = jnp.zeros((cols, slabs * LANES - middle), BF16)
            r_ref[imag, :middle] = jnp.zeros((cols, middle), BF16)
            r_ref[imag, middle:] = x_ref[own, middle:]

    x = x_ref[...]
    for u in range(0, slabs, 2):
        r = r_ref[2 * u * cols : (2 * u + 4) * cols, :]
        cross = lax.dot_general(x, r, (((1,), (1,)), ((), ())), preferred_element_type=F32)
        for v in range(2):
            part = cross[:, v * LANES : (v + 1) * LANES]
            out_ref[:, u + v] = part.astype(BF16).reshape(chans, rows, LANES)


def cross_spectra(got):
    chans, slabs, rows, lanes = got.shape
    return pl.pallas_call(
        cross_kernel,
        out_shape=jax.ShapeDtypeStruct(got.shape, BF16),
        in_specs=[VMEM],
        out_specs=VMEM,
        scratch_shapes=[
            pltpu.VMEM((chans * rows, slabs * lanes), BF16),
            pltpu.VMEM((2 * chans * rows, slabs * lanes), BF16),
        ],
        compiler_params=pltpu.CompilerParams(vmem_limit_bytes=32 << 20),
        name="cross_spectra",
    )(got)


def body(traces, live_channel, valid_segment):
    span = traces.shape[1]
    chans, slabs = lax.axis_size("chan"), lax.axis_size("tm")
    up = [(i, i + 1) for i in range(slabs - 1)]
    down = [(j, i) for i, j in up]
    before = lax.ppermute(traces[:, span - LANES :], "tm", up)
    after = lax.ppermute(traces[:, :LANES], "tm", down)
    sent = front(traces, before, after, live_channel, valid_segment)
    got = lax.all_to_all(sent, ALL, 0, 0, tiled=True)
    pieces = cross_spectra(got.reshape(chans, slabs, *got.shape[1:]))
    back = lax.all_to_all(pieces.reshape(got.shape), ALL, 0, 0, tiled=True)
    rows, cols = back.shape[1], back.shape[2] // 2
    back = back.reshape(BINS, rows, 2, cols).astype(F32)
    count = back[0, :, 0] + back[0, :, 1]
    lagged = jnp.einsum(
        "fikj,fkl->ijl",
        back,
        jnp.asarray(inverse_tables()),
        precision=lax.Precision.HIGHEST,
        preferred_element_type=F32,
    )
    return lagged * (2.0 / jnp.maximum(count, 1.0))[:, :, None]


def solution(mesh):
    return jax.shard_map(
        body,
        mesh=mesh,
        in_specs=(P("chan", "tm"), P("chan"), P("chan", "tm")),
        out_specs=P("chan", "tm", None),
        check_vma=False,
    )
```

```python
import jax
import jax.numpy as jnp
import numpy as np
from jax import lax
from jax.experimental import pallas as pl
from jax.experimental.pallas import tpu as pltpu
from jax.sharding import PartitionSpec as P

SEG_LEN = 256
BINS = 128
HALF_WIN = 64
SMOOTH = 4
LANES = 128
ALL = ("chan", "tm")
F32 = jnp.float32
BF16 = jnp.bfloat16
VMEM = pl.BlockSpec(memory_space=pltpu.VMEM)


def split(table):
    high = table.astype(BF16)
    low = (table - high.astype(np.float32)).astype(BF16)
    return high, low


def front_tables():
    t_in = np.arange(SEG_LEN)[:, None]
    t_out = np.arange(SEG_LEN)[None, :]
    box_mid = (np.abs(t_in - t_out) <= HALF_WIN).astype(BF16)
    edge = np.arange(LANES)[:, None]
    edge = np.where(edge < HALF_WIN, SEG_LEN + edge, edge - LANES)
    box_edge = (np.abs(edge - t_out) <= HALF_WIN).astype(BF16)
    phase = 2.0 * np.pi / SEG_LEN * (t_in * np.arange(BINS)[None, :] % SEG_LEN)
    forward = np.concatenate([np.cos(phase), -np.sin(phase)], axis=1).astype(np.float32)
    bins = np.arange(BINS)
    band = (np.abs(bins[:, None] - bins[None, :]) <= SMOOTH).astype(BF16)
    band = np.concatenate([band, np.ones((BINS, BINS), BF16)], axis=1)
    return np.stack([box_mid, np.tile(box_edge, (2, 1)), *split(forward), np.tile(band, (2, 1))])


def inverse_tables():
    freq = np.arange(BINS)[:, None]
    lag = np.arange(SEG_LEN)[None, :] - BINS
    phase = 2.0 * np.pi / SEG_LEN * (freq * lag % SEG_LEN)
    table = np.stack([np.cos(phase), -np.sin(phase)], axis=1) * (freq > 0)[:, None, :]
    return table.astype(np.float32)


def mxu(a, b):
    return jnp.dot(a, b, preferred_element_type=F32)


def halves(x):
    high = x.astype(BF16)
    return high, (x - high.astype(F32)).astype(BF16)


def level(x, rim, table_ref):
    mid, edge = table_ref[0], table_ref[1]
    a_high, a_low = halves(jnp.abs(x))
    e_both = jnp.concatenate(halves(jnp.abs(rim)), axis=1)
    total = mxu(a_high, mid) + mxu(a_low, mid) + mxu(e_both, edge)
    return halves(x / (total * (1.0 / (2 * HALF_WIN + 1)) + 1e-05))


def transform(high, low, table_ref):
    table = table_ref[2]
    spec = mxu(high, table) + mxu(low, table) + mxu(high, table_ref[3])
    re, im = spec[:, :BINS], spec[:, BINS:]
    return re, im, jnp.concatenate(halves(re * re + im * im), axis=1)


def whiten(re, im, power, table_ref):
    sums = mxu(power, table_ref[4])
    floor = sums[:, :BINS] * (1.0 / (2 * SMOOTH + 1)) + sums[:, BINS:] * (0.1 / BINS)
    scale = lax.rsqrt(floor + 1e-06)
    first = lax.broadcasted_iota(jnp.int32, re.shape, 1) == 0
    return jnp.where(first, 1.0, re * scale), jnp.where(first, 0.0, im * scale)


def beside(right, left):
    lane = lax.broadcasted_iota(jnp.int32, right.shape, 1)
    return jnp.where(lane < HALF_WIN, right, left)


GROUP = 8
PIECES = 4
END = SEG_LEN + LANES


def spectra_kernel(x_hbm, table_hbm, re_ref, im_ref, head_ref, x_ref, table_ref, sems):
    rows, span = x_ref.shape
    segs = span // SEG_LEN
    width = span // PIECES
    copies = [
        pltpu.make_async_copy(
            x_hbm.at[:, g * width : (g + 1) * width],
            x_ref.at[:, g * width : (g + 1) * width],
            sems.at[g],
        )
        for g in range(PIECES)
    ]
    table_copy = pltpu.make_async_copy(table_hbm, table_ref, sems.at[PIECES])
    copies[0].start()
    table_copy.start()
    for copy in copies[1:]:
        copy.start()
    arrived = 0
    table_copy.wait()
    starts = list(range(1, segs - 1, GROUP))
    normed, spec = {}, {}
    for g in range(len(starts) + 2):
        if g < len(starts):
            own, rim = [], []
            stop = min(starts[g] + GROUP, segs - 1)
            while arrived * width < stop * SEG_LEN + LANES:
                for copy in copies[arrived : arrived + 2]:
                    copy.wait()
                arrived += 2
            for s in range(starts[g], stop):
                first, last = s * SEG_LEN, (s + 1) * SEG_LEN
                own.append(x_ref[:, first:last])
                rim.append(
                    beside(x_ref[:, last : last + LANES], x_ref[:, first - LANES : first])
                )
            normed[g] = level(
                jnp.concatenate(own, axis=0), jnp.concatenate(rim, axis=0), table_ref
            )
        if 0 <= g - 1 < len(starts):
            spec[g - 1] = transform(*normed.pop(g - 1), table_ref)
        if 0 <= g - 2:
            re, im = whiten(*spec.pop(g - 2), table_ref)
            first = (starts[g - 2] + 1) * rows
            at = slice(first, first + re.shape[0])
            re_ref[at, :] = re
            im_ref[at, :] = im
    head_ref[...] = x_ref[:, :END]


def spectra(traces, table):
    rows, span = traces.shape
    segs = span // SEG_LEN
    half = jax.ShapeDtypeStruct((segs * rows, BINS), F32)
    return pl.pallas_call(
        spectra_kernel,
        out_shape=(half, half, jax.ShapeDtypeStruct((rows, END), F32)),
        in_specs=[pl.BlockSpec(memory_space=pltpu.HBM)] * 2,
        out_specs=(VMEM, VMEM, VMEM),
        scratch_shapes=[
            pltpu.VMEM(traces.shape, F32),
            pltpu.VMEM(table.shape, BF16),
            pltpu.SemaphoreType.DMA((PIECES + 1,)),
        ],
        compiler_params=pltpu.CompilerParams(vmem_limit_bytes=32 << 20),
        name="spectra",
    )(
        pltpu.with_memory_space_constraint(traces, pltpu.HBM),
        pltpu.with_memory_space_constraint(table, pltpu.HBM),
    )


def turn_kernel(
    re_ref, im_ref, head_ref, before_ref, live_ref, valid_ref, table_ref, out_ref, turned_ref
):
    rows = head_ref.shape[0]
    segs = re_ref.shape[0] // rows
    joined = jnp.where(lax.axis_index("tm") > 0, 1.0, 0.0)
    x = jnp.concatenate([before_ref[:, LANES:END], head_ref[:, :SEG_LEN]], axis=0)
    rim = [
        beside(head_ref[:, :LANES] * joined, before_ref[:, :LANES]),
        beside(head_ref[:, SEG_LEN:END], before_ref[:, SEG_LEN:END] * joined),
    ]
    fixed = level(x, jnp.concatenate(rim, axis=0), table_ref)
    fixed = whiten(*transform(*fixed, table_ref), table_ref)
    row = lax.broadcasted_iota(jnp.int32, (8, BINS), 0)
    for c in range(rows):
        pieces = []
        for ref, ends in zip((re_ref, im_ref), fixed):
            picked = ref[pl.ds(c, segs, stride=rows), :]
            top = jnp.where(row == 1, ends[rows + c : rows + c + 1], picked[:8])
            pieces += [jnp.where(row == 0, ends[c : c + 1], top), picked[8:]]
        turned_ref[pl.ds(c, BINS, stride=rows), :] = jnp.concatenate(pieces, axis=0).T
    live = jnp.broadcast_to(live_ref[...].astype(F32), (rows, rows))
    here = [lax.broadcasted_iota(jnp.int32, (rows, rows), axis) for axis in range(2)]
    live = jnp.sum(jnp.where(here[0] == here[1], live, 0.0), axis=1, keepdims=True)
    valid = valid_ref[...].astype(F32)
    valid = jnp.concatenate([valid, valid], axis=1)
    lane = lax.broadcasted_iota(jnp.int32, valid.shape, 1)
    other = before_ref[:, :LANES]
    other = jnp.where(lane < segs, other, pltpu.roll(other, segs, 1))
    mask = live * pltpu.roll(jnp.where(lane % segs == segs - 1, other, valid), 1, 1)
    whitened = turned_ref[...].reshape(BINS, rows, LANES) * mask[None]
    out_ref[...] = whitened.astype(BF16)


def turn(parts, before, live, valid, table):
    rows, segs = valid.shape
    return pl.pallas_call(
        turn_kernel,
        out_shape=jax.ShapeDtypeStruct((BINS, rows, 2 * segs), BF16),
        in_specs=[VMEM] * 7,
        out_specs=VMEM,
        scratch_shapes=[pltpu.VMEM((BINS * rows, LANES), F32)],
        compiler_params=pltpu.CompilerParams(vmem_limit_bytes=32 << 20),
        name="turn",
    )(*parts, before, live[None, :], valid, table)


def front(traces, live, valid):
    slabs, span = lax.axis_size("tm"), traces.shape[1]
    tail = traces[:, span - END :]
    bits = jnp.pad(valid, ((0, 0), (0, END - valid.shape[1]))).astype(F32)
    tail = jnp.where(lax.broadcasted_iota(jnp.int32, tail.shape, 1) < valid.shape[1], bits, tail)
    before = lax.ppermute(tail, "tm", [(i, (i + 1) % slabs) for i in range(slabs)])
    table = jnp.asarray(front_tables())
    return turn(spectra(traces, table), before, live, valid, table)


def cross_kernel(got_ref, out_ref, x_ref, r_ref):
    chans, slabs, rows, _ = got_ref.shape
    cols = chans * rows // slabs
    half = LANES // 2
    lane = lax.broadcasted_iota(jnp.int32, (chans * rows, LANES), 1)
    sign = jnp.where(lane < half, 1.0, -1.0)
    for t in range(slabs):
        tile = got_ref[:, t].reshape(chans * rows, LANES)
        turned = (pltpu.roll(tile.astype(F32), half, 1) * sign).astype(BF16)
        at = slice(t * LANES, (t + 1) * LANES)
        x_ref[:, at] = tile
        for u in range(slabs):
            r_ref[2 * u * cols : (2 * u + 1) * cols, at] = tile[u * cols : (u + 1) * cols]
            r_ref[(2 * u + 1) * cols : (2 * u + 2) * cols, at] = turned[u * cols : (u + 1) * cols]
    middle = slabs // 2 * LANES

    @pl.when(lax.axis_index("chan") * lax.axis_size("tm") + lax.axis_index("tm") == 0)
    def _():
        for u in range(slabs):
            real = slice(2 * u * cols, (2 * u + 1) * cols)
            imag = slice((2 * u + 1) * cols, (2 * u + 2) * cols)
            own = slice(u * cols, (u + 1) * cols)
            r_ref[real, middle:] = jnp.zeros((cols, slabs * LANES - middle), BF16)
            r_ref[imag, :middle] = jnp.zeros((cols, middle), BF16)
            r_ref[imag, middle:] = x_ref[own, middle:]

    x = x_ref[...]
    for u in range(0, slabs, 2):
        r = r_ref[2 * u * cols : (2 * u + 4) * cols, :]
        cross = lax.dot_general(x, r, (((1,), (1,)), ((), ())), preferred_element_type=F32)
        for v in range(2):
            part = cross[:, v * LANES : (v + 1) * LANES]
            out_ref[:, u + v] = part.astype(BF16).reshape(chans, rows, LANES)


def cross_spectra(got):
    chans, slabs, rows, lanes = got.shape
    return pl.pallas_call(
        cross_kernel,
        out_shape=jax.ShapeDtypeStruct(got.shape, BF16),
        in_specs=[VMEM],
        out_specs=VMEM,
        scratch_shapes=[
            pltpu.VMEM((chans * rows, slabs * lanes), BF16),
            pltpu.VMEM((2 * chans * rows, slabs * lanes), BF16),
        ],
        compiler_params=pltpu.CompilerParams(vmem_limit_bytes=32 << 20),
        name="cross_spectra",
    )(got)


def body(traces, live_channel, valid_segment):
    chans, slabs = lax.axis_size("chan"), lax.axis_size("tm")
    sent = front(traces, live_channel, valid_segment)
    got = lax.all_to_all(sent, ALL, 0, 0, tiled=True)
    pieces = cross_spectra(got.reshape(chans, slabs, *got.shape[1:]))
    back = lax.all_to_all(pieces.reshape(got.shape), ALL, 0, 0, tiled=True)
    rows, cols = back.shape[1], back.shape[2] // 2
    back = back.reshape(BINS, rows, 2, cols).astype(F32)
    count = back[0, :, 0] + back[0, :, 1]
    lagged = jnp.einsum(
        "fikj,fkl->ijl",
        back,
        jnp.asarray(inverse_tables()),
        precision=lax.Precision.HIGHEST,
        preferred_element_type=F32,
    )
    return lagged * (2.0 / jnp.maximum(count, 1.0))[:, :, None]


def solution(mesh):
    return jax.shard_map(
        body,
        mesh=mesh,
        in_specs=(P("chan", "tm"), P("chan"), P("chan", "tm")),
        out_specs=P("chan", "tm", None),
        check_vma=False,
    )
```

```python
import jax
import jax.numpy as jnp
import numpy as np
from jax import lax
from jax.experimental import pallas as pl
from jax.experimental.pallas import tpu as pltpu
from jax.sharding import PartitionSpec as P

SEG_LEN = 256
BINS = 128
HALF_WIN = 64
SMOOTH = 4
LANES = 128
ALL = ("chan", "tm")
F32 = jnp.float32
BF16 = jnp.bfloat16
VMEM = pl.BlockSpec(memory_space=pltpu.VMEM)


def split(table):
    high = table.astype(BF16)
    low = (table - high.astype(np.float32)).astype(BF16)
    return high, low


def front_tables():
    t_in = np.arange(SEG_LEN)[:, None]
    t_out = np.arange(SEG_LEN)[None, :]
    box_mid = (np.abs(t_in - t_out) <= HALF_WIN).astype(BF16)
    edge = np.arange(LANES)[:, None]
    edge = np.where(edge < HALF_WIN, SEG_LEN + edge, edge - LANES)
    box_edge = (np.abs(edge - t_out) <= HALF_WIN).astype(BF16)
    phase = 2.0 * np.pi / SEG_LEN * (t_in * np.arange(BINS)[None, :] % SEG_LEN)
    forward = np.concatenate([np.cos(phase), -np.sin(phase)], axis=1).astype(np.float32)
    bins = np.arange(BINS)
    band = (np.abs(bins[:, None] - bins[None, :]) <= SMOOTH).astype(BF16)
    band = np.concatenate([band, np.ones((BINS, BINS), BF16)], axis=1)
    return np.stack([box_mid, np.tile(box_edge, (2, 1)), *split(forward), np.tile(band, (2, 1))])


def inverse_table():
    freq = np.arange(BINS)[:, None]
    lag = np.arange(SEG_LEN)[None, :] - BINS
    phase = 2.0 * np.pi / SEG_LEN * (freq * lag % SEG_LEN)
    table = np.concatenate([np.cos(phase), -np.sin(phase)], axis=0).astype(np.float32)
    table = table * np.tile(freq > 0, (2, 1))
    count = np.broadcast_to(np.tile(freq == 0, (2, 1)), (2 * BINS, LANES)).astype(BF16)
    return np.concatenate([*split(table), count], axis=1)


def mxu(a, b):
    return jnp.dot(a, b, preferred_element_type=F32)


def halves(x):
    high = x.astype(BF16)
    return high, (x - high.astype(F32)).astype(BF16)


def level(x, rim, table_ref):
    mid, edge = table_ref[0], table_ref[1]
    a_high, a_low = halves(jnp.abs(x))
    e_both = jnp.concatenate(halves(jnp.abs(rim)), axis=1)
    total = mxu(a_high, mid) + mxu(a_low, mid) + mxu(e_both, edge)
    return halves(x / (total * (1.0 / (2 * HALF_WIN + 1)) + 1e-05))


def transform(high, low, table_ref):
    table = table_ref[2]
    spec = mxu(high, table) + mxu(low, table) + mxu(high, table_ref[3])
    re, im = spec[:, :BINS], spec[:, BINS:]
    return re, im, jnp.concatenate(halves(re * re + im * im), axis=1)


def whiten(re, im, power, table_ref):
    sums = mxu(power, table_ref[4])
    floor = sums[:, :BINS] * (1.0 / (2 * SMOOTH + 1)) + sums[:, BINS:] * (0.1 / BINS)
    scale = lax.rsqrt(floor + 1e-06)
    first = lax.broadcasted_iota(jnp.int32, re.shape, 1) == 0
    return jnp.where(first, 1.0, re * scale), jnp.where(first, 0.0, im * scale)


def beside(right, left):
    lane = lax.broadcasted_iota(jnp.int32, right.shape, 1)
    return jnp.where(lane < HALF_WIN, right, left)


GROUP = 8
PIECES = 4
PAD = 4
END = SEG_LEN + LANES


def spectra_kernel(x_hbm, table_hbm, re_ref, im_ref, head_ref, x_ref, table_ref, sems):
    rows, span = x_ref.shape
    segs = span // SEG_LEN
    width = span // PIECES
    copies = [
        pltpu.make_async_copy(
            x_hbm.at[:, g * width : (g + 1) * width],
            x_ref.at[:, g * width : (g + 1) * width],
            sems.at[g],
        )
        for g in range(PIECES)
    ]
    table_copy = pltpu.make_async_copy(table_hbm, table_ref, sems.at[PIECES])
    copies[0].start()
    table_copy.start()
    for copy in copies[1:]:
        copy.start()
    arrived = 0
    table_copy.wait()
    starts = list(range(1, segs - 1, GROUP))
    normed, spec = {}, {}
    for g in range(len(starts) + 2):
        if g < len(starts):
            own, rim = [], []
            stop = min(starts[g] + GROUP, segs - 1)
            while arrived * width < stop * SEG_LEN + LANES:
                for copy in copies[arrived : arrived + 2]:
                    copy.wait()
                arrived += 2
            for s in range(starts[g], stop):
                first, last = s * SEG_LEN, (s + 1) * SEG_LEN
                own.append(x_ref[:, first:last])
                rim.append(
                    beside(x_ref[:, last : last + LANES], x_ref[:, first - LANES : first])
                )
            normed[g] = level(
                jnp.concatenate(own, axis=0), jnp.concatenate(rim, axis=0), table_ref
            )
        if 0 <= g - 1 < len(starts):
            spec[g - 1] = transform(*normed.pop(g - 1), table_ref)
        if 0 <= g - 2:
            re, im = whiten(*spec.pop(g - 2), table_ref)
            for s in range(re.shape[0] // rows):
                first = (starts[g - 2] + 1 + s) * (rows + PAD)
                re_ref[first : first + rows, :] = re[s * rows : (s + 1) * rows]
                im_ref[first : first + rows, :] = im[s * rows : (s + 1) * rows]
    head_ref[...] = x_ref[:, :END]


def spectra(traces, table):
    rows, span = traces.shape
    segs = span // SEG_LEN
    half = jax.ShapeDtypeStruct((segs * (rows + PAD), BINS), F32)
    return pl.pallas_call(
        spectra_kernel,
        out_shape=(half, half, jax.ShapeDtypeStruct((rows, END), F32)),
        in_specs=[pl.BlockSpec(memory_space=pltpu.HBM)] * 2,
        out_specs=(VMEM, VMEM, VMEM),
        scratch_shapes=[
            pltpu.VMEM(traces.shape, F32),
            pltpu.VMEM(table.shape, BF16),
            pltpu.SemaphoreType.DMA((PIECES + 1,)),
        ],
        compiler_params=pltpu.CompilerParams(vmem_limit_bytes=32 << 20),
        name="spectra",
    )(
        pltpu.with_memory_space_constraint(traces, pltpu.HBM),
        pltpu.with_memory_space_constraint(table, pltpu.HBM),
    )


def turn_kernel(
    re_ref, im_ref, head_ref, before_ref, live_ref, valid_ref, table_ref, out_ref, turned_ref
):
    rows = head_ref.shape[0]
    segs = valid_ref.shape[1]
    joined = jnp.where(lax.axis_index("tm") > 0, 1.0, 0.0)
    x = jnp.concatenate([before_ref[:, LANES:END], head_ref[:, :SEG_LEN]], axis=0)
    rim = [
        beside(head_ref[:, :LANES] * joined, before_ref[:, :LANES]),
        beside(head_ref[:, SEG_LEN:END], before_ref[:, SEG_LEN:END] * joined),
    ]
    fixed = level(x, jnp.concatenate(rim, axis=0), table_ref)
    fixed = whiten(*transform(*fixed, table_ref), table_ref)
    row = lax.broadcasted_iota(jnp.int32, (8, BINS), 0)
    for c in range(rows):
        pieces = []
        for ref, ends in zip((re_ref, im_ref), fixed):
            picked = ref[pl.ds(c, segs, stride=rows + PAD), :]
            top = jnp.where(row == 1, ends[rows + c : rows + c + 1], picked[:8])
            pieces += [jnp.where(row == 0, ends[c : c + 1], top), picked[8:]]
        turned_ref[pl.ds(c, BINS, stride=rows + PAD), :] = jnp.concatenate(pieces, axis=0).T
    live = jnp.broadcast_to(live_ref[...].astype(F32), (rows, rows))
    here = [lax.broadcasted_iota(jnp.int32, (rows, rows), axis) for axis in range(2)]
    live = jnp.sum(jnp.where(here[0] == here[1], live, 0.0), axis=1, keepdims=True)
    valid = valid_ref[...].astype(F32)
    valid = jnp.concatenate([valid, valid], axis=1)
    lane = lax.broadcasted_iota(jnp.int32, valid.shape, 1)
    other = before_ref[:, :LANES]
    other = jnp.where(lane < segs, other, pltpu.roll(other, segs, 1))
    mask = live * pltpu.roll(jnp.where(lane % segs == segs - 1, other, valid), 1, 1)
    for f in range(BINS):
        first = f * (rows + PAD)
        out_ref[f] = (turned_ref[first : first + rows, :] * mask).astype(BF16)


def turn(parts, before, live, valid, table):
    rows, segs = valid.shape
    return pl.pallas_call(
        turn_kernel,
        out_shape=jax.ShapeDtypeStruct((BINS, rows, 2 * segs), BF16),
        in_specs=[VMEM] * 7,
        out_specs=VMEM,
        scratch_shapes=[pltpu.VMEM((BINS * (rows + PAD), LANES), F32)],
        compiler_params=pltpu.CompilerParams(vmem_limit_bytes=32 << 20),
        name="turn",
    )(*parts, before, live[None, :], valid, table)


def front(traces, live, valid):
    slabs, span = lax.axis_size("tm"), traces.shape[1]
    tail = traces[:, span - END :]
    bits = jnp.pad(valid, ((0, 0), (0, END - valid.shape[1]))).astype(F32)
    tail = jnp.where(lax.broadcasted_iota(jnp.int32, tail.shape, 1) < valid.shape[1], bits, tail)
    before = lax.ppermute(tail, "tm", [(i, (i + 1) % slabs) for i in range(slabs)])
    table = jnp.asarray(front_tables())
    return turn(spectra(traces, table), before, live, valid, table)


def cross_kernel(got_ref, out_ref, x_ref, r_ref):
    chans, slabs, rows, _ = got_ref.shape
    cols = chans * rows // slabs
    half = LANES // 2
    lane = lax.broadcasted_iota(jnp.int32, (chans * rows, LANES), 1)
    sign = jnp.where(lane < half, 1.0, -1.0)
    for t in range(slabs):
        tile = got_ref[:, t].reshape(chans * rows, LANES)
        turned = (pltpu.roll(tile.astype(F32), half, 1) * sign).astype(BF16)
        at = slice(t * LANES, (t + 1) * LANES)
        x_ref[:, at] = tile
        for u in range(slabs):
            r_ref[2 * u * cols : (2 * u + 1) * cols, at] = tile[u * cols : (u + 1) * cols]
            r_ref[(2 * u + 1) * cols : (2 * u + 2) * cols, at] = turned[u * cols : (u + 1) * cols]
    middle = slabs // 2 * LANES

    @pl.when(lax.axis_index("chan") * lax.axis_size("tm") + lax.axis_index("tm") == 0)
    def _():
        for u in range(slabs):
            real = slice(2 * u * cols, (2 * u + 1) * cols)
            imag = slice((2 * u + 1) * cols, (2 * u + 2) * cols)
            own = slice(u * cols, (u + 1) * cols)
            r_ref[real, middle:] = jnp.zeros((cols, slabs * LANES - middle), BF16)
            r_ref[imag, :middle] = jnp.zeros((cols, middle), BF16)
            r_ref[imag, middle:] = x_ref[own, middle:]

    x = x_ref[...]
    for u in range(0, slabs, 2):
        r = r_ref[2 * u * cols : (2 * u + 4) * cols, :]
        cross = lax.dot_general(x, r, (((1,), (1,)), ((), ())), preferred_element_type=F32)
        for v in range(2):
            part = cross[:, v * LANES : (v + 1) * LANES]
            out_ref[:, u + v] = part.astype(BF16).reshape(chans, rows, LANES)


def cross_spectra(got):
    chans, slabs, rows, lanes = got.shape
    return pl.pallas_call(
        cross_kernel,
        out_shape=jax.ShapeDtypeStruct(got.shape, BF16),
        in_specs=[VMEM],
        out_specs=VMEM,
        scratch_shapes=[
            pltpu.VMEM((chans * rows, slabs * lanes), BF16),
            pltpu.VMEM((2 * chans * rows, slabs * lanes), BF16),
        ],
        compiler_params=pltpu.CompilerParams(vmem_limit_bytes=32 << 20),
        name="cross_spectra",
    )(got)


def inverse_kernel(back_ref, table_ref, out_hbm, turned_ref, out_ref, sems):
    _, rows, lanes = back_ref.shape
    cols = lanes // 2
    for f in range(BINS):
        turned_ref[f * (rows + PAD) : f * (rows + PAD) + rows, :] = back_ref[f].astype(F32)
    groups = rows // GROUP
    pieces = {}
    copies = []
    for g in range(groups + 1):
        if g < groups:
            piece = []
            for i in range(g * GROUP, (g + 1) * GROUP):
                turned = turned_ref[pl.ds(i, BINS, stride=rows + PAD), :].T.astype(BF16)
                piece.append(jnp.concatenate([turned[:cols], turned[cols:]], axis=1))
            pieces[g] = jnp.concatenate(piece, axis=0)
        if g > 0:
            full = mxu(pieces.pop(g - 1), table_ref[...])
            scale = 2.0 / jnp.maximum(full[:, 2 * SEG_LEN :], 1.0)
            lagged = full[:, :SEG_LEN] + full[:, SEG_LEN : 2 * SEG_LEN]
            lagged = lagged * jnp.concatenate([scale, scale], axis=1)
            at = slice((g - 1) * GROUP, g * GROUP)
            out_ref[at] = lagged.reshape(GROUP, cols, SEG_LEN)
            copies.append(pltpu.make_async_copy(out_ref.at[at], out_hbm.at[at], sems.at[g - 1]))
            copies[-1].start()
    for copy in copies:
        copy.wait()


def inverse(back):
    bins, rows, lanes = back.shape
    shape = (rows, lanes // 2, SEG_LEN)
    return pl.pallas_call(
        inverse_kernel,
        out_shape=jax.ShapeDtypeStruct(shape, F32),
        in_specs=[VMEM, VMEM],
        out_specs=pl.BlockSpec(memory_space=pltpu.HBM),
        scratch_shapes=[
            pltpu.VMEM((bins * (rows + PAD), lanes), F32),
            pltpu.VMEM(shape, F32),
            pltpu.SemaphoreType.DMA((rows // GROUP,)),
        ],
        compiler_params=pltpu.CompilerParams(vmem_limit_bytes=32 << 20),
        name="inverse",
    )(back, jnp.asarray(inverse_table()))


def body(traces, live_channel, valid_segment):
    chans, slabs = lax.axis_size("chan"), lax.axis_size("tm")
    sent = front(traces, live_channel, valid_segment)
    got = lax.all_to_all(sent, ALL, 0, 0, tiled=True)
    pieces = cross_spectra(got.reshape(chans, slabs, *got.shape[1:]))
    back = lax.all_to_all(pieces.reshape(got.shape), ALL, 0, 0, tiled=True)
    return inverse(back)


def solution(mesh):
    return jax.shard_map(
        body,
        mesh=mesh,
        in_specs=(P("chan", "tm"), P("chan"), P("chan", "tm")),
        out_specs=P("chan", "tm", None),
        check_vma=False,
    )
```

```python
import jax
import jax.numpy as jnp
import numpy as np
from jax import lax
from jax.experimental import pallas as pl
from jax.experimental.pallas import tpu as pltpu
from jax.sharding import PartitionSpec as P

SEG_LEN = 256
BINS = 128
HALF_WIN = 64
SMOOTH = 4
LANES = 128
ALL = ("chan", "tm")
F32 = jnp.float32
BF16 = jnp.bfloat16
VMEM = pl.BlockSpec(memory_space=pltpu.VMEM)


def split(table):
    high = table.astype(BF16)
    low = (table - high.astype(np.float32)).astype(BF16)
    return high, low


def front_tables():
    t_in = np.arange(SEG_LEN)[:, None]
    t_out = np.arange(SEG_LEN)[None, :]
    box_mid = (np.abs(t_in - t_out) <= HALF_WIN).astype(BF16)
    edge = np.arange(LANES)[:, None]
    edge = np.where(edge < HALF_WIN, SEG_LEN + edge, edge - LANES)
    box_edge = (np.abs(edge - t_out) <= HALF_WIN).astype(BF16)
    phase = 2.0 * np.pi / SEG_LEN * (t_in * np.arange(BINS)[None, :] % SEG_LEN)
    forward = np.concatenate([np.cos(phase), -np.sin(phase)], axis=1).astype(np.float32)
    bins = np.arange(BINS)
    band = (np.abs(bins[:, None] - bins[None, :]) <= SMOOTH).astype(BF16)
    band = np.concatenate([band, np.ones((BINS, BINS), BF16)], axis=1)
    return np.stack([box_mid, np.tile(box_edge, (2, 1)), *split(forward), np.tile(band, (2, 1))])


def inverse_table():
    freq = np.arange(BINS)[:, None]
    lag = np.arange(SEG_LEN)[None, :] - BINS
    phase = 2.0 * np.pi / SEG_LEN * (freq * lag % SEG_LEN)
    table = np.concatenate([np.cos(phase), -np.sin(phase)], axis=0).astype(np.float32)
    table = table * np.tile(freq > 0, (2, 1))
    count = np.broadcast_to(np.tile(freq == 0, (2, 1)), (2 * BINS, LANES)).astype(BF16)
    return np.concatenate([*split(table), count], axis=1)


def mxu(a, b):
    return jnp.dot(a, b, preferred_element_type=F32)


def halves(x):
    high = x.astype(BF16)
    return high, (x - high.astype(F32)).astype(BF16)


def level(x, rim, table_ref):
    mid, edge = table_ref[0], table_ref[1]
    a_high, a_low = halves(jnp.abs(x))
    e_both = jnp.concatenate(halves(jnp.abs(rim)), axis=1)
    total = mxu(a_high, mid) + mxu(a_low, mid) + mxu(e_both, edge)
    return halves(x / (total * (1.0 / (2 * HALF_WIN + 1)) + 1e-05))


def transform(high, low, table_ref):
    table = table_ref[2]
    spec = mxu(high, table) + mxu(low, table) + mxu(high, table_ref[3])
    re, im = spec[:, :BINS], spec[:, BINS:]
    return re, im, jnp.concatenate(halves(re * re + im * im), axis=1)


def whiten(re, im, power, table_ref):
    sums = mxu(power, table_ref[4])
    floor = sums[:, :BINS] * (1.0 / (2 * SMOOTH + 1)) + sums[:, BINS:] * (0.1 / BINS)
    scale = lax.rsqrt(floor + 1e-06)
    first = lax.broadcasted_iota(jnp.int32, re.shape, 1) == 0
    return jnp.where(first, 1.0, re * scale), jnp.where(first, 0.0, im * scale)


def beside(right, left):
    lane = lax.broadcasted_iota(jnp.int32, right.shape, 1)
    return jnp.where(lane < HALF_WIN, right, left)


GROUP = 8
PIECES = 4
PAD = 4
END = SEG_LEN + LANES


def spectra_kernel(x_hbm, table_hbm, re_ref, im_ref, head_ref, x_ref, table_ref, sems):
    rows, span = x_ref.shape
    segs = span // SEG_LEN
    width = span // PIECES
    copies = [
        pltpu.make_async_copy(
            x_hbm.at[:, g * width : (g + 1) * width],
            x_ref.at[:, g * width : (g + 1) * width],
            sems.at[g],
        )
        for g in range(PIECES)
    ]
    table_copy = pltpu.make_async_copy(table_hbm, table_ref, sems.at[PIECES])
    copies[0].start()
    table_copy.start()
    for copy in copies[1:]:
        copy.start()
    arrived = 0
    table_copy.wait()
    starts = list(range(1, segs - 1, GROUP))
    normed, spec = {}, {}
    for g in range(len(starts) + 2):
        if g < len(starts):
            own, rim = [], []
            stop = min(starts[g] + GROUP, segs - 1)
            while arrived * width < stop * SEG_LEN + LANES:
                for copy in copies[arrived : arrived + 2]:
                    copy.wait()
                arrived += 2
            for s in range(starts[g], stop):
                first, last = s * SEG_LEN, (s + 1) * SEG_LEN
                own.append(x_ref[:, first:last])
                rim.append(
                    beside(x_ref[:, last : last + LANES], x_ref[:, first - LANES : first])
                )
            normed[g] = level(
                jnp.concatenate(own, axis=0), jnp.concatenate(rim, axis=0), table_ref
            )
        if 0 <= g - 1 < len(starts):
            spec[g - 1] = transform(*normed.pop(g - 1), table_ref)
        if 0 <= g - 2:
            re, im = whiten(*spec.pop(g - 2), table_ref)
            for s in range(re.shape[0] // rows):
                first = (starts[g - 2] + 1 + s) * (rows + PAD)
                re_ref[first : first + rows, :] = re[s * rows : (s + 1) * rows]
                im_ref[first : first + rows, :] = im[s * rows : (s + 1) * rows]
    head_ref[...] = x_ref[:, :END]


def spectra(traces, table):
    rows, span = traces.shape
    segs = span // SEG_LEN
    half = jax.ShapeDtypeStruct((segs * (rows + PAD), BINS), F32)
    return pl.pallas_call(
        spectra_kernel,
        out_shape=(half, half, jax.ShapeDtypeStruct((rows, END), F32)),
        in_specs=[pl.BlockSpec(memory_space=pltpu.HBM)] * 2,
        out_specs=(VMEM, VMEM, VMEM),
        scratch_shapes=[
            pltpu.VMEM(traces.shape, F32),
            pltpu.VMEM(table.shape, BF16),
            pltpu.SemaphoreType.DMA((PIECES + 1,)),
        ],
        compiler_params=pltpu.CompilerParams(vmem_limit_bytes=32 << 20),
        name="spectra",
    )(
        pltpu.with_memory_space_constraint(traces, pltpu.HBM),
        pltpu.with_memory_space_constraint(table, pltpu.HBM),
    )


def turn_kernel(
    re_ref, im_ref, head_ref, before_ref, live_ref, valid_ref, table_ref, out_ref, turned_ref
):
    rows = head_ref.shape[0]
    segs = valid_ref.shape[1]
    joined = jnp.where(lax.axis_index("tm") > 0, 1.0, 0.0)
    x = jnp.concatenate([before_ref[:, LANES:END], head_ref[:, :SEG_LEN]], axis=0)
    rim = [
        beside(head_ref[:, :LANES] * joined, before_ref[:, :LANES]),
        beside(head_ref[:, SEG_LEN:END], before_ref[:, SEG_LEN:END] * joined),
    ]
    fixed = level(x, jnp.concatenate(rim, axis=0), table_ref)
    fixed = whiten(*transform(*fixed, table_ref), table_ref)
    row = lax.broadcasted_iota(jnp.int32, (8, BINS), 0)
    for c in range(rows):
        pieces = []
        for ref, ends in zip((re_ref, im_ref), fixed):
            picked = ref[pl.ds(c, segs, stride=rows + PAD), :]
            top = jnp.where(row == 1, ends[rows + c : rows + c + 1], picked[:8])
            pieces += [jnp.where(row == 0, ends[c : c + 1], top), picked[8:]]
        turned_ref[pl.ds(c, BINS, stride=rows + PAD), :] = jnp.concatenate(pieces, axis=0).T
    live = jnp.broadcast_to(live_ref[...].astype(F32), (rows, rows))
    here = [lax.broadcasted_iota(jnp.int32, (rows, rows), axis) for axis in range(2)]
    live = jnp.sum(jnp.where(here[0] == here[1], live, 0.0), axis=1, keepdims=True)
    valid = valid_ref[...].astype(F32)
    valid = jnp.concatenate([valid, valid], axis=1)
    lane = lax.broadcasted_iota(jnp.int32, valid.shape, 1)
    other = before_ref[:, :LANES]
    other = jnp.where(lane < segs, other, pltpu.roll(other, segs, 1))
    mask = live * pltpu.roll(jnp.where(lane % segs == segs - 1, other, valid), 1, 1)
    for f in range(BINS):
        first = f * (rows + PAD)
        out_ref[f] = (turned_ref[first : first + rows, :] * mask).astype(BF16)


def turn(parts, before, live, valid, table):
    rows, segs = valid.shape
    return pl.pallas_call(
        turn_kernel,
        out_shape=jax.ShapeDtypeStruct((BINS, rows, 2 * segs), BF16),
        in_specs=[VMEM] * 7,
        out_specs=VMEM,
        scratch_shapes=[pltpu.VMEM((BINS * (rows + PAD), LANES), F32)],
        compiler_params=pltpu.CompilerParams(vmem_limit_bytes=32 << 20),
        name="turn",
    )(*parts, before, live[None, :], valid, table)


def front(traces, live, valid):
    slabs, span = lax.axis_size("tm"), traces.shape[1]
    tail = traces[:, span - END :]
    bits = jnp.pad(valid, ((0, 0), (0, END - valid.shape[1]))).astype(F32)
    tail = jnp.where(lax.broadcasted_iota(jnp.int32, tail.shape, 1) < valid.shape[1], bits, tail)
    before = lax.ppermute(tail, "tm", [(i, (i + 1) % slabs) for i in range(slabs)])
    table = jnp.asarray(front_tables())
    return turn(spectra(traces, table), before, live, valid, table)


def cross_kernel(got_ref, out_ref, x_ref, r_ref):
    chans, slabs, rows, _ = got_ref.shape
    cols = chans * rows // slabs
    blocks = chans // slabs
    half = LANES // 2
    counts = lax.axis_index("chan") * lax.axis_size("tm") + lax.axis_index("tm") == 0
    kept = jnp.where(counts, 0.0, 1.0)
    lane = lax.broadcasted_iota(jnp.int32, (cols, LANES), 1)
    sign = jnp.where(lane < half, kept, -kept).astype(BF16)
    moved = jnp.full((cols, LANES), 1.0 - kept).astype(BF16)
    kept = jnp.full((cols, LANES), kept).astype(BF16)
    for t in range(slabs):
        at = slice(t * LANES, (t + 1) * LANES)
        x_ref[:, at] = got_ref[:, t].reshape(chans * rows, LANES)
    for u in range(0, slabs + 2, 2):
        for v in range(u, min(u + 2, slabs)):
            own = slice(v * blocks, (v + 1) * blocks)
            for t in range(slabs):
                at = slice(t * LANES, (t + 1) * LANES)
                tile = got_ref[own, t].reshape(cols, LANES)
                turned = pltpu.roll(tile, half, 1) * sign
                if t >= slabs // 2:
                    turned = turned + tile * moved
                    tile = tile * kept
                r_ref[2 * v * cols : (2 * v + 1) * cols, at] = tile
                r_ref[(2 * v + 1) * cols : (2 * v + 2) * cols, at] = turned
        if u == 0:
            continue
        r = r_ref[2 * (u - 2) * cols : 2 * u * cols, :]
        cross = lax.dot_general(
            x_ref[...], r, (((1,), (1,)), ((), ())), preferred_element_type=F32
        )
        for v in range(2):
            part = cross[:, v * LANES : (v + 1) * LANES]
            out_ref[:, u - 2 + v] = part.astype(BF16).reshape(chans, rows, LANES)


def cross_spectra(got):
    chans, slabs, rows, lanes = got.shape
    return pl.pallas_call(
        cross_kernel,
        out_shape=jax.ShapeDtypeStruct(got.shape, BF16),
        in_specs=[VMEM],
        out_specs=VMEM,
        scratch_shapes=[
            pltpu.VMEM((chans * rows, slabs * lanes), BF16),
            pltpu.VMEM((2 * chans * rows, slabs * lanes), BF16),
        ],
        compiler_params=pltpu.CompilerParams(vmem_limit_bytes=32 << 20),
        name="cross_spectra",
    )(got)


ROWS = 4


def inverse_kernel(back_ref, table_ref, out_hbm, turned_ref, out_ref, sems):
    _, rows, lanes = back_ref.shape
    cols = lanes // 2
    for f in range(BINS):
        turned_ref[f * (rows + PAD) : f * (rows + PAD) + rows, :] = back_ref[f].astype(F32)
    groups = rows // ROWS
    pieces = {}
    copies = []
    for g in range(groups + 1):
        if g < groups:
            piece = []
            for i in range(g * ROWS, (g + 1) * ROWS):
                turned = turned_ref[pl.ds(i, BINS, stride=rows + PAD), :].T.astype(BF16)
                piece.append(jnp.concatenate([turned[:cols], turned[cols:]], axis=1))
            pieces[g] = jnp.concatenate(piece, axis=0)
        if g > 0:
            full = mxu(pieces.pop(g - 1), table_ref[...])
            scale = 2.0 / jnp.maximum(full[:, 2 * SEG_LEN :], 1.0)
            lagged = full[:, :SEG_LEN] + full[:, SEG_LEN : 2 * SEG_LEN]
            lagged = lagged * jnp.concatenate([scale, scale], axis=1)
            at = slice((g - 1) * ROWS, g * ROWS)
            out_ref[at] = lagged.reshape(ROWS, cols, SEG_LEN)
            copies.append(pltpu.make_async_copy(out_ref.at[at], out_hbm.at[at], sems.at[g - 1]))
            copies[-1].start()
    for copy in copies:
        copy.wait()


def inverse(back):
    bins, rows, lanes = back.shape
    shape = (rows, lanes // 2, SEG_LEN)
    return pl.pallas_call(
        inverse_kernel,
        out_shape=jax.ShapeDtypeStruct(shape, F32),
        in_specs=[VMEM, VMEM],
        out_specs=pl.BlockSpec(memory_space=pltpu.HBM),
        scratch_shapes=[
            pltpu.VMEM((bins * (rows + PAD), lanes), F32),
            pltpu.VMEM(shape, F32),
            pltpu.SemaphoreType.DMA((rows // ROWS,)),
        ],
        compiler_params=pltpu.CompilerParams(vmem_limit_bytes=32 << 20),
        name="inverse",
    )(back, jnp.asarray(inverse_table()))


def body(traces, live_channel, valid_segment):
    chans, slabs = lax.axis_size("chan"), lax.axis_size("tm")
    sent = front(traces, live_channel, valid_segment)
    got = lax.all_to_all(sent, ALL, 0, 0, tiled=True)
    pieces = cross_spectra(got.reshape(chans, slabs, *got.shape[1:]))
    back = lax.all_to_all(pieces.reshape(got.shape), ALL, 0, 0, tiled=True)
    return inverse(back)


def solution(mesh):
    return jax.shard_map(
        body,
        mesh=mesh,
        in_specs=(P("chan", "tm"), P("chan"), P("chan", "tm")),
        out_specs=P("chan", "tm", None),
        check_vma=False,
    )
```

```python
import jax
import jax.numpy as jnp
import numpy as np
from jax import lax
from jax.experimental import pallas as pl
from jax.experimental.pallas import tpu as pltpu
from jax.sharding import PartitionSpec as P

SEG_LEN = 256
BINS = 128
HALF_WIN = 64
SMOOTH = 4
LANES = 128
ALL = ("chan", "tm")
F32 = jnp.float32
BF16 = jnp.bfloat16
VMEM = pl.BlockSpec(memory_space=pltpu.VMEM)
ORDER = np.concatenate([np.arange(0, BINS, 2), np.arange(1, BINS, 2)])


def split(table):
    high = table.astype(BF16)
    low = (table - high.astype(np.float32)).astype(BF16)
    return high, low


def front_tables():
    t_in = np.arange(SEG_LEN)[:, None]
    t_out = np.arange(SEG_LEN)[None, :]
    box_mid = (np.abs(t_in - t_out) <= HALF_WIN).astype(BF16)
    edge = np.arange(LANES)[:, None]
    edge = np.where(edge < HALF_WIN, SEG_LEN + edge, edge - LANES)
    box_edge = (np.abs(edge - t_out) <= HALF_WIN).astype(BF16)
    phase = 2.0 * np.pi / SEG_LEN * (np.arange(LANES)[:, None] * ORDER[None, :] % SEG_LEN)
    real, imag = np.cos(phase), -np.sin(phase)
    half = BINS // 2
    even = split(np.concatenate([real[:, :half], imag[:, :half]], axis=1).astype(np.float32))
    odd = split(np.concatenate([imag[:, half:], real[:, half:]], axis=1).astype(np.float32))
    even, odd = (np.tile(np.concatenate(both, axis=1), (2, 1)) for both in (even, odd))
    band = (np.abs(ORDER[:, None] - ORDER[None, :]) <= SMOOTH).astype(BF16)
    band = np.concatenate([band, np.ones((BINS, BINS), BF16)], axis=1)
    return np.stack([box_mid, np.tile(box_edge, (2, 1)), even, odd, np.tile(band, (2, 1))])


def inverse_table():
    freq = ORDER[:, None]
    lag = np.arange(SEG_LEN)[None, :] - BINS
    phase = 2.0 * np.pi / SEG_LEN * (freq * lag % SEG_LEN)
    table = np.concatenate([np.cos(phase), -np.sin(phase)], axis=0).astype(np.float32)
    table = table * np.tile(freq > 0, (2, 1))
    count = np.broadcast_to(np.tile(freq == 0, (2, 1)), (2 * BINS, LANES)).astype(BF16)
    return np.concatenate([*split(table), count], axis=1)


def mxu(a, b):
    return jnp.dot(a, b, preferred_element_type=F32)


def halves(x):
    high = x.astype(BF16)
    return high, (x - high.astype(F32)).astype(BF16)


def level(x, rim, table_ref):
    mid, edge = table_ref[0], table_ref[1]
    a_high, a_low = halves(jnp.abs(x))
    e_both = jnp.concatenate(halves(jnp.abs(rim)), axis=1)
    total = mxu(a_high, mid) + mxu(a_low, mid) + mxu(e_both, edge)
    normed = x / (total * (1.0 / (2 * HALF_WIN + 1)) + 1e-05)
    head, tail = normed[:, :LANES], normed[:, LANES:]
    return [jnp.concatenate(halves(part), axis=1) for part in (head + tail, head - tail)]


def transform(sums, differences, table_ref):
    even, odd = mxu(sums, table_ref[2]), mxu(differences, table_ref[3])
    even = even[:, :LANES] + even[:, LANES:]
    odd = odd[:, :LANES] + odd[:, LANES:]
    front = lax.broadcasted_iota(jnp.int32, even.shape, 1) < BINS // 2
    re = jnp.where(front, even, odd)
    im = pltpu.roll(jnp.where(front, odd, even), BINS // 2, 1)
    return re, im, jnp.concatenate(halves(re * re + im * im), axis=1)


def whiten(re, im, power, table_ref):
    sums = mxu(power, table_ref[4])
    floor = sums[:, :BINS] * (1.0 / (2 * SMOOTH + 1)) + sums[:, BINS:] * (0.1 / BINS)
    scale = lax.rsqrt(floor + 1e-06)
    first = lax.broadcasted_iota(jnp.int32, re.shape, 1) == 0
    return jnp.where(first, 1.0, re * scale), jnp.where(first, 0.0, im * scale)


def beside(right, left):
    lane = lax.broadcasted_iota(jnp.int32, right.shape, 1)
    return jnp.where(lane < HALF_WIN, right, left)


GROUP = 8
PIECES = 4
PAD = 4
END = SEG_LEN + LANES


def spectra_kernel(x_hbm, table_hbm, re_ref, im_ref, head_ref, x_ref, table_ref, sems):
    rows, span = x_ref.shape
    segs = span // SEG_LEN
    width = span // PIECES
    copies = [
        pltpu.make_async_copy(
            x_hbm.at[:, g * width : (g + 1) * width],
            x_ref.at[:, g * width : (g + 1) * width],
            sems.at[g],
        )
        for g in range(PIECES)
    ]
    table_copy = pltpu.make_async_copy(table_hbm, table_ref, sems.at[PIECES])
    copies[0].start()
    table_copy.start()
    for copy in copies[1:]:
        copy.start()
    arrived = 0
    table_copy.wait()
    starts = list(range(1, segs - 1, GROUP))
    normed, spec = {}, {}
    for g in range(len(starts) + 2):
        if g < len(starts):
            own, rim = [], []
            stop = min(starts[g] + GROUP, segs - 1)
            while arrived * width < stop * SEG_LEN + LANES:
                for copy in copies[arrived : arrived + 2]:
                    copy.wait()
                arrived += 2
            for s in range(starts[g], stop):
                first, last = s * SEG_LEN, (s + 1) * SEG_LEN
                own.append(x_ref[:, first:last])
                rim.append(
                    beside(x_ref[:, last : last + LANES], x_ref[:, first - LANES : first])
                )
            normed[g] = level(
                jnp.concatenate(own, axis=0), jnp.concatenate(rim, axis=0), table_ref
            )
        if 0 <= g - 1 < len(starts):
            spec[g - 1] = transform(*normed.pop(g - 1), table_ref)
        if 0 <= g - 2:
            re, im = whiten(*spec.pop(g - 2), table_ref)
            for s in range(re.shape[0] // rows):
                first = (starts[g - 2] + 1 + s) * (rows + PAD)
                re_ref[first : first + rows, :] = re[s * rows : (s + 1) * rows]
                im_ref[first : first + rows, :] = im[s * rows : (s + 1) * rows]
    head_ref[...] = x_ref[:, :END]


def spectra(traces, table):
    rows, span = traces.shape
    segs = span // SEG_LEN
    half = jax.ShapeDtypeStruct((segs * (rows + PAD), BINS), F32)
    return pl.pallas_call(
        spectra_kernel,
        out_shape=(half, half, jax.ShapeDtypeStruct((rows, END), F32)),
        in_specs=[pl.BlockSpec(memory_space=pltpu.HBM)] * 2,
        out_specs=(VMEM, VMEM, VMEM),
        scratch_shapes=[
            pltpu.VMEM(traces.shape, F32),
            pltpu.VMEM(table.shape, BF16),
            pltpu.SemaphoreType.DMA((PIECES + 1,)),
        ],
        compiler_params=pltpu.CompilerParams(vmem_limit_bytes=32 << 20),
        name="spectra",
    )(
        pltpu.with_memory_space_constraint(traces, pltpu.HBM),
        pltpu.with_memory_space_constraint(table, pltpu.HBM),
    )


def turn_kernel(
    re_ref, im_ref, head_ref, before_ref, live_ref, valid_ref, table_ref, out_ref, turned_ref
):
    rows = head_ref.shape[0]
    segs = valid_ref.shape[1]
    joined = jnp.where(lax.axis_index("tm") > 0, 1.0, 0.0)
    x = jnp.concatenate([before_ref[:, LANES:END], head_ref[:, :SEG_LEN]], axis=0)
    rim = [
        beside(head_ref[:, :LANES] * joined, before_ref[:, :LANES]),
        beside(head_ref[:, SEG_LEN:END], before_ref[:, SEG_LEN:END] * joined),
    ]
    fixed = level(x, jnp.concatenate(rim, axis=0), table_ref)
    fixed = whiten(*transform(*fixed, table_ref), table_ref)
    row = lax.broadcasted_iota(jnp.int32, (8, BINS), 0)
    for c in range(rows):
        pieces = []
        for ref, ends in zip((re_ref, im_ref), fixed):
            picked = ref[pl.ds(c, segs, stride=rows + PAD), :]
            top = jnp.where(row == 1, ends[rows + c : rows + c + 1], picked[:8])
            pieces += [jnp.where(row == 0, ends[c : c + 1], top), picked[8:]]
        turned_ref[pl.ds(c, BINS, stride=rows + PAD), :] = jnp.concatenate(pieces, axis=0).T
    live = jnp.broadcast_to(live_ref[...].astype(F32), (rows, rows))
    here = [lax.broadcasted_iota(jnp.int32, (rows, rows), axis) for axis in range(2)]
    live = jnp.sum(jnp.where(here[0] == here[1], live, 0.0), axis=1, keepdims=True)
    valid = valid_ref[...].astype(F32)
    valid = jnp.concatenate([valid, valid], axis=1)
    lane = lax.broadcasted_iota(jnp.int32, valid.shape, 1)
    other = before_ref[:, :LANES]
    other = jnp.where(lane < segs, other, pltpu.roll(other, segs, 1))
    mask = live * pltpu.roll(jnp.where(lane % segs == segs - 1, other, valid), 1, 1)
    for f in range(BINS):
        first = f * (rows + PAD)
        out_ref[f] = (turned_ref[first : first + rows, :] * mask).astype(BF16)


def turn(parts, before, live, valid, table):
    rows, segs = valid.shape
    return pl.pallas_call(
        turn_kernel,
        out_shape=jax.ShapeDtypeStruct((BINS, rows, 2 * segs), BF16),
        in_specs=[VMEM] * 7,
        out_specs=VMEM,
        scratch_shapes=[pltpu.VMEM((BINS * (rows + PAD), LANES), F32)],
        compiler_params=pltpu.CompilerParams(vmem_limit_bytes=32 << 20),
        name="turn",
    )(*parts, before, live[None, :], valid, table)


def front(traces, live, valid):
    slabs, span = lax.axis_size("tm"), traces.shape[1]
    tail = traces[:, span - END :]
    bits = jnp.pad(valid, ((0, 0), (0, END - valid.shape[1]))).astype(F32)
    tail = jnp.where(lax.broadcasted_iota(jnp.int32, tail.shape, 1) < valid.shape[1], bits, tail)
    before = lax.ppermute(tail, "tm", [(i, (i + 1) % slabs) for i in range(slabs)])
    table = jnp.asarray(front_tables())
    return turn(spectra(traces, table), before, live, valid, table)


def cross_kernel(got_ref, out_ref, x_ref, r_ref):
    chans, slabs, rows, _ = got_ref.shape
    cols = chans * rows // slabs
    blocks = chans // slabs
    half = LANES // 2
    counts = lax.axis_index("chan") * lax.axis_size("tm") + lax.axis_index("tm") == 0
    kept = jnp.where(counts, 0.0, 1.0)
    lane = lax.broadcasted_iota(jnp.int32, (cols, LANES), 1)
    sign = jnp.where(lane < half, kept, -kept).astype(BF16)
    moved = jnp.full((cols, LANES), 1.0 - kept).astype(BF16)
    kept = jnp.full((cols, LANES), kept).astype(BF16)
    for t in range(slabs):
        at = slice(t * LANES, (t + 1) * LANES)
        x_ref[:, at] = got_ref[:, t].reshape(chans * rows, LANES)
    for u in range(0, slabs + 2, 2):
        for v in range(u, min(u + 2, slabs)):
            own = slice(v * blocks, (v + 1) * blocks)
            for t in range(slabs):
                at = slice(t * LANES, (t + 1) * LANES)
                tile = got_ref[own, t].reshape(cols, LANES)
                turned = pltpu.roll(tile, half, 1) * sign
                if t >= slabs // 2:
                    turned = turned + tile * moved
                    tile = tile * kept
                r_ref[2 * v * cols : (2 * v + 1) * cols, at] = tile
                r_ref[(2 * v + 1) * cols : (2 * v + 2) * cols, at] = turned
        if u == 0:
            continue
        r = r_ref[2 * (u - 2) * cols : 2 * u * cols, :]
        cross = lax.dot_general(
            x_ref[...], r, (((1,), (1,)), ((), ())), preferred_element_type=F32
        )
        for v in range(2):
            part = cross[:, v * LANES : (v + 1) * LANES]
            out_ref[:, u - 2 + v] = part.astype(BF16).reshape(chans, rows, LANES)


def cross_spectra(got):
    chans, slabs, rows, lanes = got.shape
    return pl.pallas_call(
        cross_kernel,
        out_shape=jax.ShapeDtypeStruct(got.shape, BF16),
        in_specs=[VMEM],
        out_specs=VMEM,
        scratch_shapes=[
            pltpu.VMEM((chans * rows, slabs * lanes), BF16),
            pltpu.VMEM((2 * chans * rows, slabs * lanes), BF16),
        ],
        compiler_params=pltpu.CompilerParams(vmem_limit_bytes=32 << 20),
        name="cross_spectra",
    )(got)


ROWS = 4


def inverse_kernel(back_ref, table_ref, out_hbm, turned_ref, out_ref, sems):
    _, rows, lanes = back_ref.shape
    cols = lanes // 2
    part = rows // 2

    def place(first, bins):
        for f in bins:
            at = f * (rows + PAD) + first
            turned_ref[at : at + part, :] = back_ref[f, first : first + part].astype(F32)

    place(0, range(BINS))
    groups = rows // ROWS
    step = BINS // (groups // 2)
    pieces = {}
    copies = []
    for g in range(groups + 1):
        if g < groups // 2:
            place(part, range(g * step, (g + 1) * step))
        if g < groups:
            piece = []
            for i in range(g * ROWS, (g + 1) * ROWS):
                turned = turned_ref[pl.ds(i, BINS, stride=rows + PAD), :].T.astype(BF16)
                piece.append(jnp.concatenate([turned[:cols], turned[cols:]], axis=1))
            pieces[g] = jnp.concatenate(piece, axis=0)
        if g > 0:
            full = mxu(pieces.pop(g - 1), table_ref[...])
            scale = 2.0 / jnp.maximum(full[:, 2 * SEG_LEN :], 1.0)
            lagged = full[:, :SEG_LEN] + full[:, SEG_LEN : 2 * SEG_LEN]
            lagged = lagged * jnp.concatenate([scale, scale], axis=1)
            at = slice((g - 1) * ROWS, g * ROWS)
            out_ref[at] = lagged.reshape(ROWS, cols, SEG_LEN)
            copies.append(pltpu.make_async_copy(out_ref.at[at], out_hbm.at[at], sems.at[g - 1]))
            copies[-1].start()
    for copy in copies:
        copy.wait()


def inverse(back):
    bins, rows, lanes = back.shape
    shape = (rows, lanes // 2, SEG_LEN)
    return pl.pallas_call(
        inverse_kernel,
        out_shape=jax.ShapeDtypeStruct(shape, F32),
        in_specs=[VMEM, VMEM],
        out_specs=pl.BlockSpec(memory_space=pltpu.HBM),
        scratch_shapes=[
            pltpu.VMEM((bins * (rows + PAD), lanes), F32),
            pltpu.VMEM(shape, F32),
            pltpu.SemaphoreType.DMA((rows // ROWS,)),
        ],
        compiler_params=pltpu.CompilerParams(vmem_limit_bytes=32 << 20),
        name="inverse",
    )(back, jnp.asarray(inverse_table()))


def body(traces, live_channel, valid_segment):
    chans, slabs = lax.axis_size("chan"), lax.axis_size("tm")
    sent = front(traces, live_channel, valid_segment)
    got = lax.all_to_all(sent, ALL, 0, 0, tiled=True)
    pieces = cross_spectra(got.reshape(chans, slabs, *got.shape[1:]))
    back = lax.all_to_all(pieces.reshape(got.shape), ALL, 0, 0, tiled=True)
    return inverse(back)


def solution(mesh):
    return jax.shard_map(
        body,
        mesh=mesh,
        in_specs=(P("chan", "tm"), P("chan"), P("chan", "tm")),
        out_specs=P("chan", "tm", None),
        check_vma=False,
    )
```

```python
import jax
import jax.numpy as jnp
import numpy as np
from jax import lax
from jax.experimental import pallas as pl
from jax.experimental.pallas import tpu as pltpu
from jax.sharding import PartitionSpec as P

SEG_LEN = 256
BINS = 128
HALF_WIN = 64
SMOOTH = 4
LANES = 128
ALL = ("chan", "tm")
F32 = jnp.float32
BF16 = jnp.bfloat16
VMEM = pl.BlockSpec(memory_space=pltpu.VMEM)
ORDER = np.concatenate([np.arange(0, BINS, 2), np.arange(1, BINS, 2)])


def split(table):
    high = table.astype(BF16)
    low = (table - high.astype(np.float32)).astype(BF16)
    return high, low


def front_tables():
    t_in = np.arange(SEG_LEN)[:, None]
    t_out = np.arange(SEG_LEN)[None, :]
    box_mid = (np.abs(t_in - t_out) <= HALF_WIN).astype(BF16)
    edge = np.arange(LANES)[:, None]
    edge = np.where(edge < HALF_WIN, SEG_LEN + edge, edge - LANES)
    box_edge = (np.abs(edge - t_out) <= HALF_WIN).astype(BF16)
    phase = 2.0 * np.pi / SEG_LEN * (np.arange(LANES)[:, None] * ORDER[None, :] % SEG_LEN)
    real, imag = np.cos(phase), -np.sin(phase)
    half = BINS // 2
    even = split(np.concatenate([real[:, :half], imag[:, :half]], axis=1).astype(np.float32))
    odd = split(np.concatenate([imag[:, half:], real[:, half:]], axis=1).astype(np.float32))
    even, odd = (np.tile(np.concatenate(both, axis=1), (2, 1)) for both in (even, odd))
    band = (np.abs(ORDER[:, None] - ORDER[None, :]) <= SMOOTH).astype(BF16)
    band = np.concatenate([band, np.ones((BINS, BINS), BF16)], axis=1)
    return np.stack([box_mid, np.tile(box_edge, (2, 1)), even, odd, np.tile(band, (2, 1))])


def inverse_table():
    freq = ORDER[:, None]
    lag = np.arange(SEG_LEN)[None, :] - BINS
    phase = 2.0 * np.pi / SEG_LEN * (freq * lag % SEG_LEN)
    table = np.concatenate([np.cos(phase), -np.sin(phase)], axis=0).astype(np.float32)
    table = table * np.tile(freq > 0, (2, 1))
    count = np.broadcast_to(np.tile(freq == 0, (2, 1)), (2 * BINS, LANES)).astype(BF16)
    return np.concatenate([*split(table), count], axis=1)


def mxu(a, b):
    return jnp.dot(a, b, preferred_element_type=F32)


def halves(x):
    high = x.astype(BF16)
    return high, (x - high.astype(F32)).astype(BF16)


def level(x, rim, table_ref):
    mid, edge = table_ref[0], table_ref[1]
    a_high, a_low = halves(jnp.abs(x))
    e_both = jnp.concatenate(halves(jnp.abs(rim)), axis=1)
    total = mxu(a_high, mid) + mxu(a_low, mid) + mxu(e_both, edge)
    normed = x / (total * (1.0 / (2 * HALF_WIN + 1)) + 1e-05)
    head, tail = normed[:, :LANES], normed[:, LANES:]
    return [jnp.concatenate(halves(part), axis=1) for part in (head + tail, head - tail)]


def transform(sums, differences, table_ref):
    even, odd = mxu(sums, table_ref[2]), mxu(differences, table_ref[3])
    even = even[:, :LANES] + even[:, LANES:]
    odd = odd[:, :LANES] + odd[:, LANES:]
    front = lax.broadcasted_iota(jnp.int32, even.shape, 1) < BINS // 2
    re = jnp.where(front, even, odd)
    im = pltpu.roll(jnp.where(front, odd, even), BINS // 2, 1)
    return re, im, jnp.concatenate(halves(re * re + im * im), axis=1)


def whiten(re, im, power, table_ref):
    sums = mxu(power, table_ref[4])
    floor = sums[:, :BINS] * (1.0 / (2 * SMOOTH + 1)) + sums[:, BINS:] * (0.1 / BINS)
    scale = lax.rsqrt(floor + 1e-06)
    return re * scale, im * scale


def beside(right, left):
    lane = lax.broadcasted_iota(jnp.int32, right.shape, 1)
    return jnp.where(lane < HALF_WIN, right, left)


GROUP = 8
PIECES = 8
PAD = 4
END = SEG_LEN + LANES
LATE = 16


def gather(ref, firsts):
    own = [ref[:, i : i + SEG_LEN] for i in firsts]
    rim = [
        beside(ref[:, i + SEG_LEN : i + SEG_LEN + LANES], ref[:, i - LANES : i]) for i in firsts
    ]
    return jnp.concatenate(own, axis=0), jnp.concatenate(rim, axis=0)


def keep(parts, refs, slot, rows):
    for part, ref in zip(parts, refs):
        for s in range(part.shape[0] // rows):
            first = (slot + s) * (rows + PAD)
            ref[first : first + rows, :] = part[s * rows : (s + 1) * rows]


def spectra_kernel(x_hbm, table_hbm, re_ref, im_ref, head_ref, rest_ref, x_ref, table_ref, sems):
    rows, span = x_ref.shape
    segs = span // SEG_LEN
    width = span // PIECES
    copies = [
        pltpu.make_async_copy(
            x_hbm.at[:, g * width : (g + 1) * width],
            x_ref.at[:, g * width : (g + 1) * width],
            sems.at[g],
        )
        for g in range(PIECES)
    ]
    box, others = (
        pltpu.make_async_copy(table_hbm.at[at], table_ref.at[at], sems.at[PIECES + i])
        for i, at in enumerate((slice(0, 2), slice(2, 5)))
    )
    needed = (GROUP + 1) * SEG_LEN + LANES
    early = -(-needed // width)
    for copy in (*copies[:early], box, *copies[early:], others):
        copy.start()
    for copy in (*copies[:early], box):
        copy.wait()
    stop = segs - 1 - LATE
    starts = list(range(1, stop, GROUP))
    normed, spec = {}, {}
    for g in range(len(starts) + 2):
        if g < len(starts):
            if g == 1:
                for copy in (*copies[early:], others):
                    copy.wait()
            firsts = [s * SEG_LEN for s in range(starts[g], min(starts[g] + GROUP, stop))]
            normed[g] = level(*gather(x_ref, firsts), table_ref)
        if 0 <= g - 1 < len(starts):
            spec[g - 1] = transform(*normed.pop(g - 1), table_ref)
        if 0 <= g - 2:
            done = whiten(*spec.pop(g - 2), table_ref)
            keep(done, (re_ref, im_ref), starts[g - 2] + 1, rows)
    head_ref[...] = x_ref[:, :END]
    rest_ref[...] = x_ref[:, stop * SEG_LEN - LANES : (segs - 1) * SEG_LEN + LANES]


def spectra(traces, table):
    rows, span = traces.shape
    segs = span // SEG_LEN
    half = jax.ShapeDtypeStruct(((segs - LATE) * (rows + PAD), BINS), F32)
    head = jax.ShapeDtypeStruct((rows, END), F32)
    rest = jax.ShapeDtypeStruct((rows, LATE * SEG_LEN + 2 * LANES), F32)
    return pl.pallas_call(
        spectra_kernel,
        out_shape=(half, half, head, rest),
        in_specs=[pl.BlockSpec(memory_space=pltpu.HBM)] * 2,
        out_specs=(VMEM,) * 4,
        scratch_shapes=[
            pltpu.VMEM(traces.shape, F32),
            pltpu.VMEM(table.shape, BF16),
            pltpu.SemaphoreType.DMA((PIECES + 2,)),
        ],
        compiler_params=pltpu.CompilerParams(vmem_limit_bytes=32 << 20),
        name="spectra",
    )(
        pltpu.with_memory_space_constraint(traces, pltpu.HBM),
        pltpu.with_memory_space_constraint(table, pltpu.HBM),
    )


def turn_kernel(
    re_ref, im_ref, head_ref, rest_ref, before_ref, live_ref, valid_ref, table_ref,
    out_ref, turned_ref, late_re_ref, late_im_ref,
):
    rows = head_ref.shape[0]
    segs = valid_ref.shape[1]
    joined = jnp.where(lax.axis_index("tm") > 0, 1.0, 0.0)
    x = jnp.concatenate([before_ref[:, LANES:END], head_ref[:, :SEG_LEN]], axis=0)
    rim = [
        beside(head_ref[:, :LANES] * joined, before_ref[:, :LANES]),
        beside(head_ref[:, SEG_LEN:END], before_ref[:, SEG_LEN:END] * joined),
    ]
    groups = [(x, jnp.concatenate(rim, axis=0))]
    for g in range(0, LATE, GROUP):
        firsts = [LANES + s * SEG_LEN for s in range(g, g + GROUP)]
        groups.append(gather(rest_ref, firsts))
    groups = [level(*group, table_ref) for group in groups]
    groups = [transform(*group, table_ref) for group in groups]
    fixed, *late = [whiten(*group, table_ref) for group in groups]
    for g, done in enumerate(late):
        keep(done, (late_re_ref, late_im_ref), g * GROUP, rows)
    row = lax.broadcasted_iota(jnp.int32, (8, BINS), 0)
    for c in range(rows):
        pieces = []
        for ref, late_ref, ends in zip((re_ref, im_ref), (late_re_ref, late_im_ref), fixed):
            picked = ref[pl.ds(c, segs - LATE, stride=rows + PAD), :]
            late = late_ref[pl.ds(c, LATE, stride=rows + PAD), :]
            top = jnp.where(row == 1, ends[rows + c : rows + c + 1], picked[:8])
            pieces += [jnp.where(row == 0, ends[c : c + 1], top), picked[8:], late]
        turned_ref[pl.ds(c, BINS, stride=rows + PAD), :] = jnp.concatenate(pieces, axis=0).T
    live = jnp.broadcast_to(live_ref[...].astype(F32), (rows, rows))
    here = [lax.broadcasted_iota(jnp.int32, (rows, rows), axis) for axis in range(2)]
    live = jnp.sum(jnp.where(here[0] == here[1], live, 0.0), axis=1, keepdims=True)
    valid = valid_ref[...].astype(F32)
    valid = jnp.concatenate([valid, valid], axis=1)
    lane = lax.broadcasted_iota(jnp.int32, valid.shape, 1)
    other = before_ref[:, :LANES]
    other = jnp.where(lane < segs, other, pltpu.roll(other, segs, 1))
    mask = live * pltpu.roll(jnp.where(lane % segs == segs - 1, other, valid), 1, 1)
    out_ref[0] = jnp.where(lane < segs, mask, 0.0).astype(BF16)
    for f in range(1, BINS):
        first = f * (rows + PAD)
        out_ref[f] = (turned_ref[first : first + rows, :] * mask).astype(BF16)


def turn(parts, before, live, valid, table):
    rows, segs = valid.shape
    return pl.pallas_call(
        turn_kernel,
        out_shape=jax.ShapeDtypeStruct((BINS, rows, 2 * segs), BF16),
        in_specs=[VMEM] * 8,
        out_specs=VMEM,
        scratch_shapes=[
            pltpu.VMEM((BINS * (rows + PAD), LANES), F32),
            pltpu.VMEM((LATE * (rows + PAD), BINS), F32),
            pltpu.VMEM((LATE * (rows + PAD), BINS), F32),
        ],
        compiler_params=pltpu.CompilerParams(vmem_limit_bytes=32 << 20),
        name="turn",
    )(*parts, before, live[None, :], valid, table)


def front(traces, live, valid):
    slabs, span = lax.axis_size("tm"), traces.shape[1]
    tail = traces[:, span - END :]
    bits = jnp.pad(valid, ((0, 0), (0, END - valid.shape[1]))).astype(F32)
    tail = jnp.where(lax.broadcasted_iota(jnp.int32, tail.shape, 1) < valid.shape[1], bits, tail)
    before = lax.ppermute(tail, "tm", [(i, (i + 1) % slabs) for i in range(slabs)])
    table = jnp.asarray(front_tables())
    return turn(spectra(traces, table), before, live, valid, table)


def cross_kernel(got_ref, out_ref, x_ref, r_ref):
    chans, slabs, rows, _ = got_ref.shape
    cols = chans * rows // slabs
    blocks = chans // slabs
    half = LANES // 2
    counts = lax.axis_index("chan") * lax.axis_size("tm") + lax.axis_index("tm") == 0
    kept = jnp.where(counts, 0.0, 1.0)
    lane = lax.broadcasted_iota(jnp.int32, (cols, LANES), 1)
    sign = jnp.where(lane < half, kept, -kept).astype(BF16)
    moved = jnp.full((cols, LANES), 1.0 - kept).astype(BF16)
    kept = jnp.full((cols, LANES), kept).astype(BF16)
    for t in range(slabs):
        at = slice(t * LANES, (t + 1) * LANES)
        x_ref[:, at] = got_ref[:, t].reshape(chans * rows, LANES)
    for u in range(0, slabs + 2, 2):
        for v in range(u, min(u + 2, slabs)):
            own = slice(v * blocks, (v + 1) * blocks)
            for t in range(slabs):
                at = slice(t * LANES, (t + 1) * LANES)
                tile = got_ref[own, t].reshape(cols, LANES)
                turned = pltpu.roll(tile, half, 1) * sign
                if t >= slabs // 2:
                    turned = turned + tile * moved
                    tile = tile * kept
                r_ref[2 * v * cols : (2 * v + 1) * cols, at] = tile
                r_ref[(2 * v + 1) * cols : (2 * v + 2) * cols, at] = turned
        if u == 0:
            continue
        r = r_ref[2 * (u - 2) * cols : 2 * u * cols, :]
        cross = lax.dot_general(
            x_ref[...], r, (((1,), (1,)), ((), ())), preferred_element_type=F32
        )
        for v in range(2):
            part = cross[:, v * LANES : (v + 1) * LANES]
            out_ref[:, u - 2 + v] = part.astype(BF16).reshape(chans, rows, LANES)


def cross_spectra(got):
    chans, slabs, rows, lanes = got.shape
    return pl.pallas_call(
        cross_kernel,
        out_shape=jax.ShapeDtypeStruct(got.shape, BF16),
        in_specs=[VMEM],
        out_specs=VMEM,
        scratch_shapes=[
            pltpu.VMEM((chans * rows, slabs * lanes), BF16),
            pltpu.VMEM((2 * chans * rows, slabs * lanes), BF16),
        ],
        compiler_params=pltpu.CompilerParams(vmem_limit_bytes=32 << 20),
        name="cross_spectra",
    )(got)


ROWS = 4


def inverse_kernel(back_ref, table_ref, out_hbm, turned_ref, out_ref, sems):
    _, rows, lanes = back_ref.shape
    cols = lanes // 2
    part = rows // 2

    def place(first, bins):
        for f in bins:
            at = f * (rows + PAD) + first
            turned_ref[at : at + part, :] = back_ref[f, first : first + part].astype(F32)

    place(0, range(BINS))
    groups = rows // ROWS
    step = BINS // (groups // 2)
    pieces = {}
    copies = []
    for g in range(groups + 1):
        if g < groups // 2:
            place(part, range(g * step, (g + 1) * step))
        if g < groups:
            piece = []
            for i in range(g * ROWS, (g + 1) * ROWS):
                turned = turned_ref[pl.ds(i, BINS, stride=rows + PAD), :].T.astype(BF16)
                piece.append(jnp.concatenate([turned[:cols], turned[cols:]], axis=1))
            pieces[g] = jnp.concatenate(piece, axis=0)
        if g > 0:
            full = mxu(pieces.pop(g - 1), table_ref[...])
            scale = 2.0 / jnp.maximum(full[:, 2 * SEG_LEN :], 1.0)
            lagged = full[:, :SEG_LEN] + full[:, SEG_LEN : 2 * SEG_LEN]
            lagged = lagged * jnp.concatenate([scale, scale], axis=1)
            at = slice((g - 1) * ROWS, g * ROWS)
            out_ref[at] = lagged.reshape(ROWS, cols, SEG_LEN)
            copies.append(pltpu.make_async_copy(out_ref.at[at], out_hbm.at[at], sems.at[g - 1]))
            copies[-1].start()
    for copy in copies:
        copy.wait()


def inverse(back):
    bins, rows, lanes = back.shape
    shape = (rows, lanes // 2, SEG_LEN)
    return pl.pallas_call(
        inverse_kernel,
        out_shape=jax.ShapeDtypeStruct(shape, F32),
        in_specs=[VMEM, VMEM],
        out_specs=pl.BlockSpec(memory_space=pltpu.HBM),
        scratch_shapes=[
            pltpu.VMEM((bins * (rows + PAD), lanes), F32),
            pltpu.VMEM(shape, F32),
            pltpu.SemaphoreType.DMA((rows // ROWS,)),
        ],
        compiler_params=pltpu.CompilerParams(vmem_limit_bytes=32 << 20),
        name="inverse",
    )(back, jnp.asarray(inverse_table()))


def body(traces, live_channel, valid_segment):
    chans, slabs = lax.axis_size("chan"), lax.axis_size("tm")
    sent = front(traces, live_channel, valid_segment)
    got = lax.all_to_all(sent, ALL, 0, 0, tiled=True)
    pieces = cross_spectra(got.reshape(chans, slabs, *got.shape[1:]))
    back = lax.all_to_all(pieces.reshape(got.shape), ALL, 0, 0, tiled=True)
    return inverse(back)


def solution(mesh):
    return jax.shard_map(
        body,
        mesh=mesh,
        in_specs=(P("chan", "tm"), P("chan"), P("chan", "tm")),
        out_specs=P("chan", "tm", None),
        check_vma=False,
    )
```

```python
import jax
import jax.numpy as jnp
import numpy as np
from jax import lax
from jax.experimental import pallas as pl
from jax.experimental.pallas import tpu as pltpu
from jax.sharding import PartitionSpec as P

SEG_LEN = 256
BINS = 128
HALF_WIN = 64
SMOOTH = 4
LANES = 128
ALL = ("chan", "tm")
F32 = jnp.float32
BF16 = jnp.bfloat16
VMEM = pl.BlockSpec(memory_space=pltpu.VMEM)
ORDER = np.concatenate([np.arange(0, BINS, 2), np.arange(1, BINS, 2)])


def split(table):
    high = table.astype(BF16)
    low = (table - high.astype(np.float32)).astype(BF16)
    return high, low


def front_tables():
    t_in = np.arange(SEG_LEN)[:, None]
    t_out = np.arange(SEG_LEN)[None, :]
    box_mid = (np.abs(t_in - t_out) <= HALF_WIN).astype(BF16)
    edge = np.arange(LANES)[:, None]
    edge = np.where(edge < HALF_WIN, SEG_LEN + edge, edge - LANES)
    box_edge = (np.abs(edge - t_out) <= HALF_WIN).astype(BF16)
    phase = 2.0 * np.pi / SEG_LEN * (np.arange(LANES)[:, None] * ORDER[None, :] % SEG_LEN)
    real, imag = np.cos(phase), -np.sin(phase)
    half = BINS // 2
    even = split(np.concatenate([real[:, :half], imag[:, :half]], axis=1).astype(np.float32))
    odd = split(np.concatenate([imag[:, half:], real[:, half:]], axis=1).astype(np.float32))
    even, odd = (np.concatenate(both, axis=1) for both in (even, odd))
    band = (np.abs(ORDER[:, None] - ORDER[None, :]) <= SMOOTH).astype(BF16)
    band = np.concatenate([band, np.ones((BINS, BINS), BF16)], axis=1)
    return np.concatenate([box_mid, box_edge, even, odd, band], axis=0)


def inverse_table():
    freq = ORDER[:, None]
    lag = np.arange(SEG_LEN)[None, :] - BINS
    phase = 2.0 * np.pi / SEG_LEN * (freq * lag % SEG_LEN)
    table = np.concatenate([np.cos(phase), -np.sin(phase)], axis=0).astype(np.float32)
    table = table * np.tile(freq > 0, (2, 1))
    count = np.broadcast_to(np.tile(freq == 0, (2, 1)), (2 * BINS, LANES)).astype(BF16)
    return np.concatenate([*split(table), count], axis=1)


def mxu(a, b):
    return jnp.dot(a, b, preferred_element_type=F32)


def halves(x):
    high = x.astype(BF16)
    return high, (x - high.astype(F32)).astype(BF16)


def twice(table_ref, block):
    table = table_ref[block * LANES : (block + 1) * LANES, :]
    return jnp.concatenate([table, table], axis=0)


def level(x, rim, table_ref):
    mid, edge = table_ref[: 2 * LANES, :], twice(table_ref, 2)
    a_high, a_low = halves(jnp.abs(x))
    e_both = jnp.concatenate(halves(jnp.abs(rim)), axis=1)
    total = mxu(a_high, mid) + mxu(a_low, mid) + mxu(e_both, edge)
    normed = x / (total * (1.0 / (2 * HALF_WIN + 1)) + 1e-05)
    head, tail = normed[:, :LANES], normed[:, LANES:]
    return [jnp.concatenate(halves(part), axis=1) for part in (head + tail, head - tail)]


def transform(sums, differences, table_ref):
    even, odd = mxu(sums, twice(table_ref, 3)), mxu(differences, twice(table_ref, 4))
    even = even[:, :LANES] + even[:, LANES:]
    odd = odd[:, :LANES] + odd[:, LANES:]
    front = lax.broadcasted_iota(jnp.int32, even.shape, 1) < BINS // 2
    re = jnp.where(front, even, odd)
    im = pltpu.roll(jnp.where(front, odd, even), BINS // 2, 1)
    return re, im, jnp.concatenate(halves(re * re + im * im), axis=1)


def whiten(re, im, power, table_ref):
    sums = mxu(power, twice(table_ref, 5))
    floor = sums[:, :BINS] * (1.0 / (2 * SMOOTH + 1)) + sums[:, BINS:] * (0.1 / BINS)
    scale = lax.rsqrt(floor + 1e-06)
    return re * scale, im * scale


def beside(right, left):
    lane = lax.broadcasted_iota(jnp.int32, right.shape, 1)
    return jnp.where(lane < HALF_WIN, right, left)


GROUP = 8
PIECES = 8
PAD = 4
END = SEG_LEN + LANES
LATE = 16


def gather(ref, firsts):
    own = [ref[:, i : i + SEG_LEN] for i in firsts]
    rim = [
        beside(ref[:, i + SEG_LEN : i + SEG_LEN + LANES], ref[:, i - LANES : i]) for i in firsts
    ]
    return jnp.concatenate(own, axis=0), jnp.concatenate(rim, axis=0)


def keep(parts, refs, slot, rows):
    for part, ref in zip(parts, refs):
        for s in range(part.shape[0] // rows):
            first = (slot + s) * (rows + PAD)
            ref[first : first + rows, :] = part[s * rows : (s + 1) * rows]


def spectra_kernel(x_hbm, table_hbm, re_ref, im_ref, head_ref, rest_ref, x_ref, table_ref, sems):
    rows, span = x_ref.shape
    segs = span // SEG_LEN
    width = span // PIECES
    copies = [
        pltpu.make_async_copy(
            x_hbm.at[:, g * width : (g + 1) * width],
            x_ref.at[:, g * width : (g + 1) * width],
            sems.at[g],
        )
        for g in range(PIECES)
    ]
    box, others = (
        pltpu.make_async_copy(table_hbm.at[at], table_ref.at[at], sems.at[PIECES + i])
        for i, at in enumerate((slice(0, 3 * LANES), slice(3 * LANES, 6 * LANES)))
    )
    needed = (GROUP + 1) * SEG_LEN + LANES
    early = -(-needed // width)
    for copy in (*copies[:early], box, *copies[early:], others):
        copy.start()
    for copy in (*copies[:early], box):
        copy.wait()
    stop = segs - 1 - LATE
    starts = list(range(1, stop, GROUP))
    normed, spec = {}, {}
    for g in range(len(starts) + 2):
        if g < len(starts):
            if g == 1:
                for copy in (*copies[early:], others):
                    copy.wait()
            firsts = [s * SEG_LEN for s in range(starts[g], min(starts[g] + GROUP, stop))]
            normed[g] = level(*gather(x_ref, firsts), table_ref)
        if 0 <= g - 1 < len(starts):
            spec[g - 1] = transform(*normed.pop(g - 1), table_ref)
        if 0 <= g - 2:
            done = whiten(*spec.pop(g - 2), table_ref)
            keep(done, (re_ref, im_ref), starts[g - 2] + 1, rows)
    head_ref[...] = x_ref[:, :END]
    rest_ref[...] = x_ref[:, stop * SEG_LEN - LANES : (segs - 1) * SEG_LEN + LANES]


def spectra(traces, table):
    rows, span = traces.shape
    segs = span // SEG_LEN
    half = jax.ShapeDtypeStruct(((segs - LATE) * (rows + PAD), BINS), F32)
    head = jax.ShapeDtypeStruct((rows, END), F32)
    rest = jax.ShapeDtypeStruct((rows, LATE * SEG_LEN + 2 * LANES), F32)
    return pl.pallas_call(
        spectra_kernel,
        out_shape=(half, half, head, rest),
        in_specs=[pl.BlockSpec(memory_space=pltpu.HBM)] * 2,
        out_specs=(VMEM,) * 4,
        scratch_shapes=[
            pltpu.VMEM(traces.shape, F32),
            pltpu.VMEM(table.shape, BF16),
            pltpu.SemaphoreType.DMA((PIECES + 2,)),
        ],
        compiler_params=pltpu.CompilerParams(vmem_limit_bytes=32 << 20),
        name="spectra",
    )(
        pltpu.with_memory_space_constraint(traces, pltpu.HBM),
        pltpu.with_memory_space_constraint(table, pltpu.HBM),
    )


def turn_kernel(
    re_ref, im_ref, head_ref, rest_ref, before_ref, live_ref, valid_ref, table_ref,
    out_ref, turned_ref, late_re_ref, late_im_ref,
):
    rows = head_ref.shape[0]
    segs = valid_ref.shape[1]
    joined = jnp.where(lax.axis_index("tm") > 0, 1.0, 0.0)
    x = jnp.concatenate([before_ref[:, LANES:END], head_ref[:, :SEG_LEN]], axis=0)
    rim = [
        beside(head_ref[:, :LANES] * joined, before_ref[:, :LANES]),
        beside(head_ref[:, SEG_LEN:END], before_ref[:, SEG_LEN:END] * joined),
    ]
    groups = [(x, jnp.concatenate(rim, axis=0))]
    for g in range(0, LATE, GROUP):
        firsts = [LANES + s * SEG_LEN for s in range(g, g + GROUP)]
        groups.append(gather(rest_ref, firsts))
    groups = [level(*group, table_ref) for group in groups]
    groups = [transform(*group, table_ref) for group in groups]
    fixed, *late = [whiten(*group, table_ref) for group in groups]
    for g, done in enumerate(late):
        keep(done, (late_re_ref, late_im_ref), g * GROUP, rows)
    row = lax.broadcasted_iota(jnp.int32, (8, BINS), 0)
    for c in range(rows):
        pieces = []
        for ref, late_ref, ends in zip((re_ref, im_ref), (late_re_ref, late_im_ref), fixed):
            picked = ref[pl.ds(c, segs - LATE, stride=rows + PAD), :]
            late = late_ref[pl.ds(c, LATE, stride=rows + PAD), :]
            top = jnp.where(row == 1, ends[rows + c : rows + c + 1], picked[:8])
            pieces += [jnp.where(row == 0, ends[c : c + 1], top), picked[8:], late]
        turned_ref[pl.ds(c, BINS, stride=rows + PAD), :] = jnp.concatenate(pieces, axis=0).T
    live = jnp.broadcast_to(live_ref[...].astype(F32), (rows, rows))
    here = [lax.broadcasted_iota(jnp.int32, (rows, rows), axis) for axis in range(2)]
    live = jnp.sum(jnp.where(here[0] == here[1], live, 0.0), axis=1, keepdims=True)
    valid = valid_ref[...].astype(F32)
    valid = jnp.concatenate([valid, valid], axis=1)
    lane = lax.broadcasted_iota(jnp.int32, valid.shape, 1)
    other = before_ref[:, :LANES]
    other = jnp.where(lane < segs, other, pltpu.roll(other, segs, 1))
    mask = live * pltpu.roll(jnp.where(lane % segs == segs - 1, other, valid), 1, 1)
    out_ref[0] = jnp.where(lane < segs, mask, 0.0).astype(BF16)
    for f in range(1, BINS):
        first = f * (rows + PAD)
        out_ref[f] = (turned_ref[first : first + rows, :] * mask).astype(BF16)


def turn(parts, before, live, valid, table):
    rows, segs = valid.shape
    return pl.pallas_call(
        turn_kernel,
        out_shape=jax.ShapeDtypeStruct((BINS, rows, 2 * segs), BF16),
        in_specs=[VMEM] * 8,
        out_specs=VMEM,
        scratch_shapes=[
            pltpu.VMEM((BINS * (rows + PAD), LANES), F32),
            pltpu.VMEM((LATE * (rows + PAD), BINS), F32),
            pltpu.VMEM((LATE * (rows + PAD), BINS), F32),
        ],
        compiler_params=pltpu.CompilerParams(vmem_limit_bytes=32 << 20),
        name="turn",
    )(*parts, before, live[None, :], valid, table)


def front(traces, live, valid):
    slabs, span = lax.axis_size("tm"), traces.shape[1]
    tail = traces[:, span - END :]
    bits = jnp.pad(valid, ((0, 0), (0, END - valid.shape[1]))).astype(F32)
    tail = jnp.where(lax.broadcasted_iota(jnp.int32, tail.shape, 1) < valid.shape[1], bits, tail)
    before = lax.ppermute(tail, "tm", [(i, (i + 1) % slabs) for i in range(slabs)])
    table = jnp.asarray(front_tables())
    return turn(spectra(traces, table), before, live, valid, table)


def cross_kernel(got_ref, out_ref, x_ref, r_ref):
    chans, slabs, rows, _ = got_ref.shape
    cols = chans * rows // slabs
    blocks = chans // slabs
    half = LANES // 2
    counts = lax.axis_index("chan") * lax.axis_size("tm") + lax.axis_index("tm") == 0
    kept = jnp.where(counts, 0.0, 1.0)
    lane = lax.broadcasted_iota(jnp.int32, (cols, LANES), 1)
    sign = jnp.where(lane < half, kept, -kept).astype(BF16)
    moved = jnp.full((cols, LANES), 1.0 - kept).astype(BF16)
    kept = jnp.full((cols, LANES), kept).astype(BF16)
    for t in range(slabs):
        at = slice(t * LANES, (t + 1) * LANES)
        x_ref[:, at] = got_ref[:, t].reshape(chans * rows, LANES)
    for u in range(0, slabs + 2, 2):
        for v in range(u, min(u + 2, slabs)):
            own = slice(v * blocks, (v + 1) * blocks)
            for t in range(slabs):
                at = slice(t * LANES, (t + 1) * LANES)
                tile = got_ref[own, t].reshape(cols, LANES)
                turned = pltpu.roll(tile, half, 1) * sign
                if t >= slabs // 2:
                    turned = turned + tile * moved
                    tile = tile * kept
                r_ref[2 * v * cols : (2 * v + 1) * cols, at] = tile
                r_ref[(2 * v + 1) * cols : (2 * v + 2) * cols, at] = turned
        if u == 0:
            continue
        r = r_ref[2 * (u - 2) * cols : 2 * u * cols, :]
        cross = lax.dot_general(
            x_ref[...], r, (((1,), (1,)), ((), ())), preferred_element_type=F32
        )
        for v in range(2):
            part = cross[:, v * LANES : (v + 1) * LANES]
            out_ref[:, u - 2 + v] = part.astype(BF16).reshape(chans, rows, LANES)


def cross_spectra(got):
    chans, slabs, rows, lanes = got.shape
    return pl.pallas_call(
        cross_kernel,
        out_shape=jax.ShapeDtypeStruct(got.shape, BF16),
        in_specs=[VMEM],
        out_specs=VMEM,
        scratch_shapes=[
            pltpu.VMEM((chans * rows, slabs * lanes), BF16),
            pltpu.VMEM((2 * chans * rows, slabs * lanes), BF16),
        ],
        compiler_params=pltpu.CompilerParams(vmem_limit_bytes=32 << 20),
        name="cross_spectra",
    )(got)


ROWS = 4


def inverse_kernel(back_ref, table_ref, out_hbm, turned_ref, out_ref, sems):
    _, rows, lanes = back_ref.shape
    cols = lanes // 2
    part = rows // 2

    def place(first, bins):
        for f in bins:
            at = f * (rows + PAD) + first
            turned_ref[at : at + part, :] = back_ref[f, first : first + part].astype(F32)

    place(0, range(BINS))
    groups = rows // ROWS
    step = BINS // (groups // 2)
    pieces = {}
    copies = []
    for g in range(groups + 1):
        if g < groups // 2:
            place(part, range(g * step, (g + 1) * step))
        if g < groups:
            piece = []
            for i in range(g * ROWS, (g + 1) * ROWS):
                turned = turned_ref[pl.ds(i, BINS, stride=rows + PAD), :].T.astype(BF16)
                piece.append(jnp.concatenate([turned[:cols], turned[cols:]], axis=1))
            pieces[g] = jnp.concatenate(piece, axis=0)
        if g > 0:
            full = mxu(pieces.pop(g - 1), table_ref[...])
            scale = 2.0 / jnp.maximum(full[:, 2 * SEG_LEN :], 1.0)
            lagged = full[:, :SEG_LEN] + full[:, SEG_LEN : 2 * SEG_LEN]
            lagged = lagged * jnp.concatenate([scale, scale], axis=1)
            at = slice((g - 1) * ROWS, g * ROWS)
            out_ref[at] = lagged.reshape(ROWS, cols, SEG_LEN)
            copies.append(pltpu.make_async_copy(out_ref.at[at], out_hbm.at[at], sems.at[g - 1]))
            copies[-1].start()
    for copy in copies:
        copy.wait()


def inverse(back):
    bins, rows, lanes = back.shape
    shape = (rows, lanes // 2, SEG_LEN)
    return pl.pallas_call(
        inverse_kernel,
        out_shape=jax.ShapeDtypeStruct(shape, F32),
        in_specs=[VMEM, VMEM],
        out_specs=pl.BlockSpec(memory_space=pltpu.HBM),
        scratch_shapes=[
            pltpu.VMEM((bins * (rows + PAD), lanes), F32),
            pltpu.VMEM(shape, F32),
            pltpu.SemaphoreType.DMA((rows // ROWS,)),
        ],
        compiler_params=pltpu.CompilerParams(vmem_limit_bytes=32 << 20),
        name="inverse",
    )(back, jnp.asarray(inverse_table()))


def body(traces, live_channel, valid_segment):
    chans, slabs = lax.axis_size("chan"), lax.axis_size("tm")
    sent = front(traces, live_channel, valid_segment)
    got = lax.all_to_all(sent, ALL, 0, 0, tiled=True)
    pieces = cross_spectra(got.reshape(chans, slabs, *got.shape[1:]))
    back = lax.all_to_all(pieces.reshape(got.shape), ALL, 0, 0, tiled=True)
    return inverse(back)


def solution(mesh):
    return jax.shard_map(
        body,
        mesh=mesh,
        in_specs=(P("chan", "tm"), P("chan"), P("chan", "tm")),
        out_specs=P("chan", "tm", None),
        check_vma=False,
    )
```

```python
import jax
import jax.numpy as jnp
import numpy as np
from jax import lax
from jax.experimental import pallas as pl
from jax.experimental.pallas import tpu as pltpu
from jax.sharding import PartitionSpec as P

SEG_LEN = 256
BINS = 128
HALF_WIN = 64
SMOOTH = 4
LANES = 128
ALL = ("chan", "tm")
F32 = jnp.float32
BF16 = jnp.bfloat16
VMEM = pl.BlockSpec(memory_space=pltpu.VMEM)
ORDER = np.concatenate([np.arange(0, BINS, 2), np.arange(1, BINS, 2)])


def split(table):
    high = table.astype(BF16)
    low = (table - high.astype(np.float32)).astype(BF16)
    return high, low


def front_tables():
    t_in = np.arange(SEG_LEN)[:, None]
    t_out = np.arange(SEG_LEN)[None, :]
    box_mid = (np.abs(t_in - t_out) <= HALF_WIN).astype(BF16)
    edge = np.arange(LANES)[:, None]
    edge = np.where(edge < HALF_WIN, SEG_LEN + edge, edge - LANES)
    box_edge = (np.abs(edge - t_out) <= HALF_WIN).astype(BF16)
    phase = 2.0 * np.pi / SEG_LEN * (np.arange(LANES)[:, None] * ORDER[None, :] % SEG_LEN)
    real, imag = np.cos(phase), -np.sin(phase)
    half = BINS // 2
    even = split(np.concatenate([real[:, :half], imag[:, :half]], axis=1).astype(np.float32))
    odd = split(np.concatenate([imag[:, half:], real[:, half:]], axis=1).astype(np.float32))
    even, odd = (np.concatenate(both, axis=1) for both in (even, odd))
    band = (np.abs(ORDER[:, None] - ORDER[None, :]) <= SMOOTH).astype(BF16)
    band = np.concatenate([band, np.ones((BINS, BINS), BF16)], axis=1)
    return np.concatenate([box_mid, box_edge, even, odd, band], axis=0)


def inverse_table():
    freq = ORDER[:, None]
    lag = np.arange(SEG_LEN)[None, :] - BINS
    phase = 2.0 * np.pi / SEG_LEN * (freq * lag % SEG_LEN)
    table = np.concatenate([np.cos(phase), -np.sin(phase)], axis=0).astype(np.float32)
    table = table * np.tile(freq > 0, (2, 1))
    count = np.broadcast_to(np.tile(freq == 0, (2, 1)), (2 * BINS, LANES)).astype(BF16)
    return np.concatenate([*split(table), count], axis=1)


def mxu(a, b):
    return jnp.dot(a, b, preferred_element_type=F32)


def halves(x):
    high = x.astype(BF16)
    return high, (x - high.astype(F32)).astype(BF16)


def twice(table_ref, block):
    table = table_ref[block * LANES : (block + 1) * LANES, :]
    return jnp.concatenate([table, table], axis=0)


def level(x, rim, table_ref):
    mid, edge = table_ref[: 2 * LANES, :], twice(table_ref, 2)
    a_high, a_low = halves(jnp.abs(x))
    e_both = jnp.concatenate(halves(jnp.abs(rim)), axis=1)
    total = mxu(a_high, mid) + mxu(a_low, mid) + mxu(e_both, edge)
    normed = x / (total * (1.0 / (2 * HALF_WIN + 1)) + 1e-05)
    head, tail = normed[:, :LANES], normed[:, LANES:]
    return [jnp.concatenate(halves(part), axis=1) for part in (head + tail, head - tail)]


def transform(sums, differences, table_ref):
    even, odd = mxu(sums, twice(table_ref, 3)), mxu(differences, twice(table_ref, 4))
    even = even[:, :LANES] + even[:, LANES:]
    odd = odd[:, :LANES] + odd[:, LANES:]
    front = lax.broadcasted_iota(jnp.int32, even.shape, 1) < BINS // 2
    re = jnp.where(front, even, odd)
    im = pltpu.roll(jnp.where(front, odd, even), BINS // 2, 1)
    return re, im, jnp.concatenate(halves(re * re + im * im), axis=1)


def whiten(re, im, power, table_ref):
    sums = mxu(power, twice(table_ref, 5))
    floor = sums[:, :BINS] * (1.0 / (2 * SMOOTH + 1)) + sums[:, BINS:] * (0.1 / BINS)
    scale = lax.rsqrt(floor + 1e-06)
    return re * scale, im * scale


def beside(right, left):
    lane = lax.broadcasted_iota(jnp.int32, right.shape, 1)
    return jnp.where(lane < HALF_WIN, right, left)


GROUP = 8
PIECES = 8
PAD = 4
END = SEG_LEN + LANES
LATE = 16


def gather(ref, firsts):
    own = [ref[:, i : i + SEG_LEN] for i in firsts]
    rim = [
        beside(ref[:, i + SEG_LEN : i + SEG_LEN + LANES], ref[:, i - LANES : i]) for i in firsts
    ]
    return jnp.concatenate(own, axis=0), jnp.concatenate(rim, axis=0)


def keep(parts, refs, slot, rows):
    for part, ref in zip(parts, refs):
        for s in range(part.shape[0] // rows):
            first = (slot + s) * (rows + PAD)
            ref[first : first + rows, :] = part[s * rows : (s + 1) * rows]


def spectra_kernel(x_hbm, table_hbm, re_ref, im_ref, head_ref, rest_ref, x_ref, table_ref, sems):
    rows, span = x_ref.shape
    segs = span // SEG_LEN
    width = span // PIECES
    copies = [
        pltpu.make_async_copy(
            x_hbm.at[:, g * width : (g + 1) * width],
            x_ref.at[:, g * width : (g + 1) * width],
            sems.at[g],
        )
        for g in range(PIECES)
    ]
    others = pltpu.make_async_copy(
        table_hbm.at[3 * LANES :], table_ref.at[3 * LANES :], sems.at[PIECES]
    )
    needed = (GROUP + 1) * SEG_LEN + LANES
    early = -(-needed // width)
    for copy in (*copies, others):
        copy.start()
    row = lax.broadcasted_iota(jnp.int32, (3 * LANES, SEG_LEN), 0)
    col = lax.broadcasted_iota(jnp.int32, (3 * LANES, SEG_LEN), 1)
    sample = jnp.where(row < SEG_LEN + HALF_WIN, row, row - (SEG_LEN + LANES))
    table_ref[: 3 * LANES, :] = jnp.where(jnp.abs(sample - col) <= HALF_WIN, 1.0, 0.0).astype(BF16)
    for copy in copies[:early]:
        copy.wait()
    stop = segs - 1 - LATE
    starts = list(range(1, stop, GROUP))
    normed, spec = {}, {}
    for g in range(len(starts) + 2):
        if g < len(starts):
            if g == 1:
                for copy in (*copies[early:], others):
                    copy.wait()
            firsts = [s * SEG_LEN for s in range(starts[g], min(starts[g] + GROUP, stop))]
            normed[g] = level(*gather(x_ref, firsts), table_ref)
        if 0 <= g - 1 < len(starts):
            spec[g - 1] = transform(*normed.pop(g - 1), table_ref)
        if 0 <= g - 2:
            done = whiten(*spec.pop(g - 2), table_ref)
            keep(done, (re_ref, im_ref), starts[g - 2] + 1, rows)
    head_ref[...] = x_ref[:, :END]
    rest_ref[...] = x_ref[:, stop * SEG_LEN - LANES : (segs - 1) * SEG_LEN + LANES]


def spectra(traces, table):
    rows, span = traces.shape
    segs = span // SEG_LEN
    half = jax.ShapeDtypeStruct(((segs - LATE) * (rows + PAD), BINS), F32)
    head = jax.ShapeDtypeStruct((rows, END), F32)
    rest = jax.ShapeDtypeStruct((rows, LATE * SEG_LEN + 2 * LANES), F32)
    return pl.pallas_call(
        spectra_kernel,
        out_shape=(half, half, head, rest),
        in_specs=[pl.BlockSpec(memory_space=pltpu.HBM)] * 2,
        out_specs=(VMEM,) * 4,
        scratch_shapes=[
            pltpu.VMEM(traces.shape, F32),
            pltpu.VMEM(table.shape, BF16),
            pltpu.SemaphoreType.DMA((PIECES + 1,)),
        ],
        compiler_params=pltpu.CompilerParams(vmem_limit_bytes=32 << 20),
        name="spectra",
    )(
        pltpu.with_memory_space_constraint(traces, pltpu.HBM),
        pltpu.with_memory_space_constraint(table, pltpu.HBM),
    )


def turn_kernel(
    re_ref, im_ref, head_ref, rest_ref, before_ref, live_ref, valid_ref, table_ref,
    out_ref, turned_ref, late_re_ref, late_im_ref,
):
    rows = head_ref.shape[0]
    segs = valid_ref.shape[1]
    joined = jnp.where(lax.axis_index("tm") > 0, 1.0, 0.0)
    x = jnp.concatenate([before_ref[:, LANES:END], head_ref[:, :SEG_LEN]], axis=0)
    rim = [
        beside(head_ref[:, :LANES] * joined, before_ref[:, :LANES]),
        beside(head_ref[:, SEG_LEN:END], before_ref[:, SEG_LEN:END] * joined),
    ]
    groups = [(x, jnp.concatenate(rim, axis=0))]
    for g in range(0, LATE, GROUP):
        firsts = [LANES + s * SEG_LEN for s in range(g, g + GROUP)]
        groups.append(gather(rest_ref, firsts))
    groups = [level(*group, table_ref) for group in groups]
    groups = [transform(*group, table_ref) for group in groups]
    fixed, *late = [whiten(*group, table_ref) for group in groups]
    for g, done in enumerate(late):
        keep(done, (late_re_ref, late_im_ref), g * GROUP, rows)
    row = lax.broadcasted_iota(jnp.int32, (8, BINS), 0)
    for c in range(rows):
        pieces = []
        for ref, late_ref, ends in zip((re_ref, im_ref), (late_re_ref, late_im_ref), fixed):
            picked = ref[pl.ds(c, segs - LATE, stride=rows + PAD), :]
            late = late_ref[pl.ds(c, LATE, stride=rows + PAD), :]
            top = jnp.where(row == 1, ends[rows + c : rows + c + 1], picked[:8])
            pieces += [jnp.where(row == 0, ends[c : c + 1], top), picked[8:], late]
        turned_ref[pl.ds(c, BINS, stride=rows + PAD), :] = jnp.concatenate(pieces, axis=0).T
    live = jnp.broadcast_to(live_ref[...].astype(F32), (rows, rows))
    here = [lax.broadcasted_iota(jnp.int32, (rows, rows), axis) for axis in range(2)]
    live = jnp.sum(jnp.where(here[0] == here[1], live, 0.0), axis=1, keepdims=True)
    valid = valid_ref[...].astype(F32)
    valid = jnp.concatenate([valid, valid], axis=1)
    lane = lax.broadcasted_iota(jnp.int32, valid.shape, 1)
    other = before_ref[:, :LANES]
    other = jnp.where(lane < segs, other, pltpu.roll(other, segs, 1))
    mask = live * pltpu.roll(jnp.where(lane % segs == segs - 1, other, valid), 1, 1)
    out_ref[0] = jnp.where(lane < segs, mask, 0.0).astype(BF16)
    for f in range(1, BINS):
        first = f * (rows + PAD)
        out_ref[f] = (turned_ref[first : first + rows, :] * mask).astype(BF16)


def turn(parts, before, live, valid, table):
    rows, segs = valid.shape
    return pl.pallas_call(
        turn_kernel,
        out_shape=jax.ShapeDtypeStruct((BINS, rows, 2 * segs), BF16),
        in_specs=[VMEM] * 8,
        out_specs=VMEM,
        scratch_shapes=[
            pltpu.VMEM((BINS * (rows + PAD), LANES), F32),
            pltpu.VMEM((LATE * (rows + PAD), BINS), F32),
            pltpu.VMEM((LATE * (rows + PAD), BINS), F32),
        ],
        compiler_params=pltpu.CompilerParams(vmem_limit_bytes=32 << 20),
        name="turn",
    )(*parts, before, live[None, :], valid, table)


def front(traces, live, valid):
    slabs, span = lax.axis_size("tm"), traces.shape[1]
    tail = traces[:, span - END :]
    bits = jnp.pad(valid, ((0, 0), (0, END - valid.shape[1]))).astype(F32)
    tail = jnp.where(lax.broadcasted_iota(jnp.int32, tail.shape, 1) < valid.shape[1], bits, tail)
    before = lax.ppermute(tail, "tm", [(i, (i + 1) % slabs) for i in range(slabs)])
    table = jnp.asarray(front_tables())
    return turn(spectra(traces, table), before, live, valid, table)


def cross_kernel(got_ref, out_ref, x_ref, r_ref):
    chans, slabs, rows, _ = got_ref.shape
    cols = chans * rows // slabs
    blocks = chans // slabs
    half = LANES // 2
    counts = lax.axis_index("chan") * lax.axis_size("tm") + lax.axis_index("tm") == 0
    kept = jnp.where(counts, 0.0, 1.0)
    lane = lax.broadcasted_iota(jnp.int32, (cols, LANES), 1)
    sign = jnp.where(lane < half, kept, -kept).astype(BF16)
    moved = jnp.full((cols, LANES), 1.0 - kept).astype(BF16)
    kept = jnp.full((cols, LANES), kept).astype(BF16)
    for t in range(slabs):
        at = slice(t * LANES, (t + 1) * LANES)
        x_ref[:, at] = got_ref[:, t].reshape(chans * rows, LANES)
    for u in range(0, slabs + 2, 2):
        for v in range(u, min(u + 2, slabs)):
            own = slice(v * blocks, (v + 1) * blocks)
            for t in range(slabs):
                at = slice(t * LANES, (t + 1) * LANES)
                tile = got_ref[own, t].reshape(cols, LANES)
                turned = pltpu.roll(tile, half, 1) * sign
                if t >= slabs // 2:
                    turned = turned + tile * moved
                    tile = tile * kept
                r_ref[2 * v * cols : (2 * v + 1) * cols, at] = tile
                r_ref[(2 * v + 1) * cols : (2 * v + 2) * cols, at] = turned
        if u == 0:
            continue
        r = r_ref[2 * (u - 2) * cols : 2 * u * cols, :]
        cross = lax.dot_general(
            x_ref[...], r, (((1,), (1,)), ((), ())), preferred_element_type=F32
        )
        for v in range(2):
            part = cross[:, v * LANES : (v + 1) * LANES]
            out_ref[:, u - 2 + v] = part.astype(BF16).reshape(chans, rows, LANES)


def cross_spectra(got):
    chans, slabs, rows, lanes = got.shape
    return pl.pallas_call(
        cross_kernel,
        out_shape=jax.ShapeDtypeStruct(got.shape, BF16),
        in_specs=[VMEM],
        out_specs=VMEM,
        scratch_shapes=[
            pltpu.VMEM((chans * rows, slabs * lanes), BF16),
            pltpu.VMEM((2 * chans * rows, slabs * lanes), BF16),
        ],
        compiler_params=pltpu.CompilerParams(vmem_limit_bytes=32 << 20),
        name="cross_spectra",
    )(got)


ROWS = 4


def inverse_kernel(back_ref, table_ref, out_hbm, turned_ref, out_ref, sems):
    _, rows, lanes = back_ref.shape
    cols = lanes // 2
    part = rows // 2

    def place(first, bins):
        for f in bins:
            at = f * (rows + PAD) + first
            turned_ref[at : at + part, :] = back_ref[f, first : first + part].astype(F32)

    place(0, range(BINS))
    groups = rows // ROWS
    step = BINS // (groups // 2)
    pieces = {}
    copies = []
    for g in range(groups + 1):
        if g < groups // 2:
            place(part, range(g * step, (g + 1) * step))
        if g < groups:
            piece = []
            for i in range(g * ROWS, (g + 1) * ROWS):
                turned = turned_ref[pl.ds(i, BINS, stride=rows + PAD), :].T.astype(BF16)
                piece.append(jnp.concatenate([turned[:cols], turned[cols:]], axis=1))
            pieces[g] = jnp.concatenate(piece, axis=0)
        if g > 0:
            full = mxu(pieces.pop(g - 1), table_ref[...])
            scale = 2.0 / jnp.maximum(full[:, 2 * SEG_LEN :], 1.0)
            lagged = full[:, :SEG_LEN] + full[:, SEG_LEN : 2 * SEG_LEN]
            lagged = lagged * jnp.concatenate([scale, scale], axis=1)
            at = slice((g - 1) * ROWS, g * ROWS)
            out_ref[at] = lagged.reshape(ROWS, cols, SEG_LEN)
            copies.append(pltpu.make_async_copy(out_ref.at[at], out_hbm.at[at], sems.at[g - 1]))
            copies[-1].start()
    for copy in copies:
        copy.wait()


def inverse(back):
    bins, rows, lanes = back.shape
    shape = (rows, lanes // 2, SEG_LEN)
    return pl.pallas_call(
        inverse_kernel,
        out_shape=jax.ShapeDtypeStruct(shape, F32),
        in_specs=[VMEM, VMEM],
        out_specs=pl.BlockSpec(memory_space=pltpu.HBM),
        scratch_shapes=[
            pltpu.VMEM((bins * (rows + PAD), lanes), F32),
            pltpu.VMEM(shape, F32),
            pltpu.SemaphoreType.DMA((rows // ROWS,)),
        ],
        compiler_params=pltpu.CompilerParams(vmem_limit_bytes=32 << 20),
        name="inverse",
    )(back, jnp.asarray(inverse_table()))


def body(traces, live_channel, valid_segment):
    chans, slabs = lax.axis_size("chan"), lax.axis_size("tm")
    sent = front(traces, live_channel, valid_segment)
    got = lax.all_to_all(sent, ALL, 0, 0, tiled=True)
    pieces = cross_spectra(got.reshape(chans, slabs, *got.shape[1:]))
    back = lax.all_to_all(pieces.reshape(got.shape), ALL, 0, 0, tiled=True)
    return inverse(back)


def solution(mesh):
    return jax.shard_map(
        body,
        mesh=mesh,
        in_specs=(P("chan", "tm"), P("chan"), P("chan", "tm")),
        out_specs=P("chan", "tm", None),
        check_vma=False,
    )
```
